512 devices in a mesh: layer: 8 (over x, z_hi), row: 8 (over y), col: 8 (over z_lo, core).
Axes of the slice: x: 4, y: 8, z: 8 (z_hi: 2, z_lo: 4; z = z_hi * 4 + z_lo), core: 2. Of those that a mesh axis runs over, the one named last changes fastest.
Arguments:
- schur_window: float32 [4, 8, 256, 2, 8, 256], P(None, 'row', None, None, 'col'), may hold values from -8 to 24, as said below
Outputs:
- factored: float32 [4, 8, 256, 2, 8, 256], P(None, 'row', 'layer', None, 'col')
The draws below stay inside these ranges and needn't reach their ends.
Inputs may be any that keep to these rules, and one draw needn't show every extreme that they name: `schur_window`: the leading 4096 columns of a symmetric positive definite matrix: its leading 4096 x 4096 block is symmetric and positive definite.
All inputs are finite; a program needn't handle non-finite values.
Results may differ from the reference program's by a relative error of at most 0.0001.
Values sent between devices are 32-bit elements; how exact they have to be, the bound alone decides.
No kernel may reach another device: no remote copies, remote signals or barrier semaphores. Data moves between devices by JAX's collectives and lax.ppermute only.
A program may use at most 64 MiB of HBM per device.

```python
import math
import jax
import jax.numpy as jnp
from jax import lax

PANEL = 256
PANELS = 2
ROW_BLOCKS = 4
COL_BLOCKS = 2
ROWS = 8192
COLS = 4096
N_ROW = 8
N_COL = 8


def draw_schur_window(key, part):
    row_total = ROW_BLOCKS * N_ROW * PANEL
    col_total = COL_BLOCKS * N_COL * PANEL
    rank_total = PANELS * PANEL
    noise_key, factor_key, diagonal_key = jax.random.split(key, 3)
    rough_part = jax.random.normal(noise_key, (row_total, col_total), jnp.float32)
    factor_draw = jax.random.normal(factor_key, (row_total, rank_total), jnp.float32)
    upper_noise = rough_part[:col_total]
    symmetric_top = (upper_noise + upper_noise.T) * 0.7071067811865476
    rough_part = jnp.concatenate([symmetric_top, rough_part[col_total:]], axis=0) * (0.25 / math.sqrt(col_total))
    coupling = jnp.dot(factor_draw, factor_draw[:col_total].T, precision=lax.Precision.HIGHEST) * (4.0 / rank_total)
    diagonal = jax.random.uniform(diagonal_key, (col_total,), jnp.float32, 2.0, 4.0)
    positions = jnp.arange(col_total, dtype=jnp.int32)
    matrix_draw = (rough_part + coupling).at[positions, positions].add(diagonal)
    return matrix_draw.reshape(ROW_BLOCKS, N_ROW, PANEL, COL_BLOCKS, N_COL, PANEL)


def setup_inputs(seed: int = 0) -> dict:
    streams_of = jax.random.split(jax.random.key(seed), 2)
    return {
        "schur_window": draw_schur_window(jax.random.fold_in(streams_of[1], 71), 0),
    }


def reference(schur_window):
    matrix = schur_window.reshape(ROWS, COLS)
    row_block = (jnp.arange(ROWS, dtype=jnp.int32) // PANEL)[:, None]
    for panel_index in range(PANELS):
        block_start = panel_index * PANEL
        block_end = block_start + PANEL
        factor = jnp.linalg.cholesky(matrix[block_start:block_end, block_start:block_end])
        solved = jax.scipy.linalg.solve_triangular(factor, matrix[:, block_start:block_end].T, lower=True).T
        column = jnp.where(row_block > panel_index, solved, jnp.zeros_like(solved))
        column = column.at[block_start:block_end].set(factor)
        update = jnp.dot(column[block_end:].astype(jnp.float32), column[block_end:COLS].T.astype(jnp.float32), precision=lax.Precision.HIGHEST, preferred_element_type=jnp.float32)
        matrix = matrix.at[block_end:, block_end:].add(-update)
        matrix = matrix.at[:, block_start:block_end].set(column)
        matrix = matrix.at[block_start:block_end, block_end:].set(jnp.zeros((PANEL, COLS - block_end), jnp.float32))
    return matrix.reshape(schur_window.shape)
```

```python
import jax
import jax.numpy as jnp
from jax import lax
from jax.experimental import pallas as pl
from jax.experimental.pallas import tpu as pltpu
from jax.sharding import PartitionSpec as P

PANELS = 2
BLOCK = 128
STRIP = 32
HIGHEST = lax.Precision.HIGHEST


def product(left, right, dims=((1,), (0,))):
    return lax.dot_general(
        left, right, (dims, ((), ())), precision=HIGHEST, preferred_element_type=jnp.float32
    )


def eliminate(groups, first_lane):
    group_count = len(groups)
    sublane = lax.broadcasted_iota(jnp.int32, (8, 128), 0)
    parts = [[group[:, :128], group[:, 128:]] for group in groups]
    finished = []
    for g in range(group_count):
        lane = first_lane + 8 * g
        heads = [
            [jnp.broadcast_to(parts[i][0][:, lane + s : lane + s + 1], (8, 128)) for s in range(8)]
            for i in range(g, group_count)
        ]
        scale = None
        for s in range(8):
            root = lax.rsqrt(jnp.broadcast_to(heads[0][s][s : s + 1, :], (8, 128)))
            inverse = root * root
            scale = root if s == 0 else jnp.where(sublane == s, root, scale)
            rows = [jnp.broadcast_to(part[s : s + 1, :], (8, 128)) for part in parts[g]]
            head_rows = [
                jnp.broadcast_to(heads[0][p][s : s + 1, :], (8, 128)) for p in range(s + 1, 8)
            ]
            for i in range(g, group_count):
                factor = heads[i - g][s] * inverse
                if i == g:
                    if s == 7:
                        continue
                    factor = jnp.where(sublane > s, factor, 0.0)
                for w in range(2):
                    parts[i][w] = parts[i][w] - factor * rows[w]
                for p in range(s + 1, 8):
                    heads[i - g][p] = heads[i - g][p] - factor * head_rows[p - s - 1]
        finished.append([part * scale for part in parts[g]])
    return [jnp.concatenate([rows[w] for rows in finished], axis=0) for w in range(2)]


def factor_kernel(a_ref, e_ref, work_ref, block_ref):
    size = a_ref.shape[0]
    block_count = size // BLOCK
    work_ref[...] = a_ref[...]
    e_ref[...] = jnp.zeros_like(e_ref)
    row_id = lax.broadcasted_iota(jnp.int32, (BLOCK, BLOCK), 0)
    col_id = lax.broadcasted_iota(jnp.int32, (BLOCK, BLOCK), 1)
    identity = (row_id == col_id).astype(jnp.float32)
    for k in range(block_count):
        begin, end = k * BLOCK, (k + 1) * BLOCK
        block_ref[:, :BLOCK] = work_ref[begin:end, begin:end]
        block_ref[:, BLOCK:] = identity
        for first in range(0, BLOCK, STRIP):
            last = first + STRIP
            groups = [block_ref[first + 8 * i : first + 8 * i + 8, :] for i in range(STRIP // 8)]
            done = eliminate(groups, first)
            both = jnp.concatenate(done, axis=1)
            block_ref[first:last, :] = both
            if last < BLOCK:
                block_ref[last:, :] -= product(done[0].T[last:], both)
        inverse = block_ref[:, BLOCK:]
        e_ref[begin:end, begin:end] = inverse
        if end < size:
            upper = product(inverse, work_ref[begin:end, end:])
            lower = upper.T
            work_ref[end:, end:] -= product(lower, upper)
        if begin > 0:
            e_ref[begin:end, :begin] = product(inverse, e_ref[begin:end, :begin])
        if end < size:
            e_ref[end:, :end] -= product(lower, e_ref[begin:end, :end])


def inverse_factor(matrix):
    size = matrix.shape[0]
    return pl.pallas_call(
        factor_kernel,
        out_shape=jax.ShapeDtypeStruct((size, size), jnp.float32),
        scratch_shapes=[
            pltpu.VMEM((size, size), jnp.float32),
            pltpu.VMEM((BLOCK, 2 * BLOCK), jnp.float32),
        ],
        name="factor",
    )(matrix)


def to_all(piece, axis, peers, groups=None):
    copies = jnp.broadcast_to(piece[None], (peers, *piece.shape))
    return lax.all_to_all(copies, axis, 0, 0, axis_index_groups=groups)


def local(schur_window):
    row_blocks, _, width, col_blocks, _, _ = schur_window.shape
    held = schur_window.reshape(row_blocks, width, col_blocks, width)
    layers = lax.axis_size("layer")
    grid_rows = lax.axis_size("row")
    grid_cols = lax.axis_size("col")
    layer_here = lax.axis_index("layer")
    row_here = lax.axis_index("row")
    col_here = lax.axis_index("col")
    x_size = layers // 2
    x_groups = [[x * 2 + z for x in range(x_size)] for z in range(2)]
    share = width // layers
    quarter = width // x_size
    lead = PANELS * width

    head = lax.dynamic_slice_in_dim(held[0], (layer_here // 2) * quarter, quarter, 0)
    quarters = to_all(head, "row", grid_rows)[:PANELS]
    gathered = to_all(quarters, "layer", x_size, x_groups)
    top = jnp.moveaxis(gathered, 0, 1).reshape(lead, col_blocks, width)

    mine = lax.dynamic_slice_in_dim(held, layer_here * share, share, 1)
    mine_first = mine[:, :, 0, :].reshape(row_blocks * share, width)
    swapped_in = jnp.concatenate([top[:, 0, :], mine_first], axis=0)
    swapped = lax.ppermute(swapped_in, "col", [(0, 1), (1, 0)])
    is_first = col_here == 0
    both = jnp.concatenate(
        [jnp.where(is_first, swapped_in, swapped), jnp.where(is_first, swapped, swapped_in)], axis=1
    )
    inverse = inverse_factor(both[:lead])
    solved = product(both[lead:], inverse, ((1,), (1,)))
    weights = product(solved, inverse)

    half = lax.dynamic_slice_in_dim(weights, (col_here % 2) * width, width, 1)
    far = lax.ppermute(half, "col", [(0, 4), (1, 5)])
    half = jnp.where(col_here < 4, half, far)
    near = lax.ppermute(half, "col", [(0, 2), (1, 3), (4, 6), (5, 7)])
    half = jnp.where(col_here % 4 < 2, half, near)
    other = lax.ppermute(half, "col", [(i, i ^ 1) for i in range(grid_cols)])
    is_even = col_here % 2 == 0
    weights_here = jnp.concatenate(
        [jnp.where(is_even, half, other), jnp.where(is_even, other, half)], axis=1
    )
    update = product(weights_here, top.reshape(lead, col_blocks * width))
    trailing = mine - update.reshape(row_blocks, share, col_blocks, width)

    row_number = (jnp.arange(row_blocks, dtype=jnp.int32) * grid_rows + row_here)[:, None, None, None]
    col_number = (jnp.arange(col_blocks, dtype=jnp.int32) * grid_cols + col_here)[None, None, :, None]
    row_inside = (jnp.arange(share, dtype=jnp.int32) + layer_here * share)[None, :, None, None]
    col_inside = jnp.arange(width, dtype=jnp.int32)[None, None, None, :]
    panel = jnp.where(is_first, solved[:, :width], solved[:, width : 2 * width])
    panel = panel.reshape(row_blocks, share, 1, width)
    below = (row_number > col_number) | ((row_number == col_number) & (row_inside >= col_inside))
    panel = jnp.where(below, panel, 0.0)
    trailing = jnp.where(row_number < PANELS, 0.0, trailing)
    result = jnp.where(col_number < PANELS, panel, trailing)
    return result.reshape(row_blocks, 1, share, col_blocks, 1, width)


def solution(mesh):
    return jax.shard_map(
        local,
        mesh=mesh,
        in_specs=(P(None, "row", None, None, "col", None),),
        out_specs=P(None, "row", "layer", None, "col", None),
        check_vma=False,
    )
```

```python
import functools
import jax
import jax.numpy as jnp
from jax import lax
from jax.experimental import pallas as pl
from jax.experimental.pallas import tpu as pltpu
from jax.sharding import PartitionSpec as P

PANELS = 2
BLOCK = 128
STRIP = 64
HIGHEST = lax.Precision.HIGHEST


def product(left, right, dims=((1,), (0,))):
    return lax.dot_general(left, right, (dims, ((), ())), precision=HIGHEST, preferred_element_type=jnp.float32)

def spread_lane(part, lane, sublane):
    return jnp.where(sublane < 8, jnp.broadcast_to(part[:, lane : lane + 1], (8, 128)), 0.0)


def eliminate(groups, first_lane, work):
    count = len(groups)
    sublane = lax.broadcasted_iota(jnp.int32, (8, 128), 0)
    lane_id = lax.broadcasted_iota(jnp.int32, (8, 128), 1)
    parts = list(groups)
    def spread(i, lane, guard):
        if guard:
            return [spread_lane(parts[i], lane + s, sublane) for s in range(8)]
        return [jnp.broadcast_to(parts[i][:, lane + s : lane + s + 1], (8, 128)) for s in range(8)]
    current = spread(0, first_lane, True)
    for g in range(count):
        lane = first_lane + 8 * g
        more = g + 1 < count
        heads = [current + (spread(g, lane + 8, True) if more else [])]
        if more:
            heads.append(spread(g + 1, lane, False) + spread(g + 1, lane + 8, True))
        for i in range(g + 2, count):
            heads.append(spread(i, lane, False))
        inside = (lane_id >= lane) & (lane_id < lane + 8)
        unit = (lane_id - lane == sublane).astype(jnp.float32)
        for i in range(g, count):
            parts[i] = jnp.where(inside, unit if i == g else 0.0, parts[i])
        scale = None
        for s in range(8):
            below = jnp.where(sublane > s, heads[0][s], 0.0)
            head_rows = [
                jnp.broadcast_to(head[s : s + 1, :], (8, 128)) for head in heads[0][s + 1 :]
            ]
            root = lax.rsqrt(jnp.broadcast_to(heads[0][s][s : s + 1, :], (8, 128)))
            inverse = root * root
            scale = root if s == 0 else jnp.where(sublane == s, root, scale)
            row = jnp.broadcast_to(parts[g][s : s + 1, :], (8, 128))
            if s < 7:
                heads[0][s + 1] = heads[0][s + 1] - (below * head_rows[0]) * inverse
            for i in range(g, count):
                if i == g and s == 7:
                    continue
                factor = (below if i == g else heads[i - g][s]) * inverse
                parts[i] = parts[i] - factor * row
                for p in range(s + 1, len(heads[i - g])):
                    if i > g or p > s + 1:
                        heads[i - g][p] = heads[i - g][p] - factor * head_rows[p - s - 1]
        parts[g] = parts[g] * scale
        if more:
            current = heads[1][8:]
        work()
    return jnp.concatenate(parts, axis=0)


def factor_kernel(first_ref, mine_ref, other_ref, v_ref, x_ref, w_ref, p_ref, e_ref, block_ref):
    size = w_ref.shape[0]
    half = size // 2
    count = size // BLOCK
    first = first_ref[0] == 1
    def left(rows):
        return jnp.where(first, mine_ref[rows, :], other_ref[rows, :])
    def right(rows):
        return jnp.where(first, other_ref[rows, :], mine_ref[rows, :])
    w_ref[:half, :half] = left(slice(0, half))
    w_ref[:, half:] = right(slice(0, size))
    p_ref[:half, :] = left(slice(size, None)).T
    p_ref[half:, :] = right(slice(size, None)).T
    row_id = lax.broadcasted_iota(jnp.int32, (BLOCK, BLOCK), 0)
    col_id = lax.broadcasted_iota(jnp.int32, (BLOCK, BLOCK), 1)
    at = [slice(k * BLOCK, (k + 1) * BLOCK) for k in range(count)]
    pending = []
    for k in range(count):
        slots = 2 * STRIP // 8
        done_slots = [0]
        per = -(-len(pending) // (slots - 2)) if pending else 0
        def work():
            done_slots[0] += 1
            for _ in range(per):
                if pending:
                    pending.pop(0)()
        block_ref[...] = w_ref[at[k], at[k]]
        for begin in range(0, BLOCK, STRIP):
            end = begin + STRIP
            groups = [block_ref[begin + 8 * i : begin + 8 * i + 8, :] for i in range(STRIP // 8)]
            done = eliminate(groups, begin, work)
            rows, lanes = row_id[begin:end], col_id[begin:end]
            block_ref[begin:end, :] = jnp.where(lanes <= rows, done, 0.0)
            if end < BLOCK:
                done = jnp.where((lanes <= rows) | (lanes >= end), done, 0.0)
                rest = block_ref[end:, :]
                rest = jnp.where((col_id[end:] >= begin) & (col_id[end:] < end), 0.0, rest)
                block_ref[end:, :] = rest - product(done.T[end:], done)
        while pending:
            pending.pop(0)()
        e_ref[at[k], at[k]] = block_ref[...]
        if k < count - 1:
            inverse = block_ref[...]
            upper = product(inverse, w_ref[at[k], at[k + 1]])
            w_ref[at[k], at[k + 1]] = upper
            w_ref[at[k + 1], at[k + 1]] -= product(upper.T, upper)
            def panel(k=k, j=0):
                w_ref[at[k], at[j]] = product(e_ref[at[k], at[k]], w_ref[at[k], at[j]])
            def panel_p(k=k):
                p_ref[at[k], :] = product(e_ref[at[k], at[k]], p_ref[at[k], :])
            def panel_e(k=k):
                e_ref[at[k], : k * BLOCK] = product(e_ref[at[k], at[k]], e_ref[at[k], : k * BLOCK])
            def trail(k=k, i=0, j=0):
                w_ref[at[i], at[j]] -= product(w_ref[at[k], at[i]].T, w_ref[at[k], at[j]])
            def trail_p(k=k, i=0):
                p_ref[at[i], :] -= product(w_ref[at[k], at[i]].T, p_ref[at[k], :])
            def trail_e(k=k, i=0):
                lower = w_ref[at[k], at[i]].T
                e_ref[at[i], at[k]] = -product(lower, e_ref[at[k], at[k]])
                if k > 0:
                    e_ref[at[i], : k * BLOCK] -= product(lower, e_ref[at[k], : k * BLOCK])
            def output(k=k):
                solved = p_ref[at[k], :].T
                v_ref[:, at[k]] = solved
                x_ref[:, at[k]] = product(solved, e_ref[at[k], at[k]])
                if k > 0:
                    x_ref[:, : k * BLOCK] += product(solved, e_ref[at[k], : k * BLOCK])
            bind = functools.partial
            for j in range(k + 2, count):
                pending.append(bind(panel, j=j))
            pending.append(bind(panel_p))
            for i in range(k + 1, count):
                for j in range(i, count):
                    if j > k + 1:
                        pending.append(bind(trail, i=i, j=j))
                pending.append(bind(trail_p, i=i))
            if k > 0:
                pending.append(bind(panel_e))
            for i in range(k + 1, count):
                pending.append(bind(trail_e, i=i))
            pending.append(bind(output))
    last = at[count - 1]
    inverse = block_ref[...]
    solved = product(p_ref[last, :], inverse, ((0,), (1,)))
    v_ref[:, last] = solved
    weights = product(solved, inverse)
    x_ref[:, last] = weights
    x_ref[:, : size - BLOCK] += product(weights, e_ref[last, : size - BLOCK])

def weigh(first, mine, other):
    size = 2 * mine.shape[1]
    share = mine.shape[0] - size
    shape = jax.ShapeDtypeStruct((share, size), jnp.float32)
    whole = pl.BlockSpec(memory_space=pltpu.VMEM)
    return pl.pallas_call(
        factor_kernel,
        out_shape=[shape, shape],
        in_specs=[pl.BlockSpec(memory_space=pltpu.SMEM), whole, whole],
        out_specs=[whole, whole],
        scratch_shapes=[
            pltpu.VMEM((size, size), jnp.float32),
            pltpu.VMEM((size, share), jnp.float32),
            pltpu.VMEM((size, size), jnp.float32),
            pltpu.VMEM((BLOCK, BLOCK), jnp.float32),
        ],
        name="factor",
    )(first, mine, other)


def to_all(piece, axis, peers, groups=None):
    copies = jnp.broadcast_to(piece[None], (peers, *piece.shape))
    return lax.all_to_all(copies, axis, 0, 0, axis_index_groups=groups)


def local(schur_window):
    row_blocks, _, width, col_blocks, _, _ = schur_window.shape
    held = schur_window.reshape(row_blocks, width, col_blocks, width)
    layers = lax.axis_size("layer")
    grid_rows = lax.axis_size("row")
    grid_cols = lax.axis_size("col")
    layer_here = lax.axis_index("layer")
    row_here = lax.axis_index("row")
    col_here = lax.axis_index("col")
    x_size = layers // 2
    x_groups = [[x * 2 + z for x in range(x_size)] for z in range(2)]
    share = width // layers
    quarter = width // x_size
    lead = PANELS * width

    head = lax.dynamic_slice(
        schur_window,
        (0, 0, (layer_here // 2) * quarter, 0, 0, 0),
        (1, 1, quarter, col_blocks, 1, width),
    ).reshape(quarter, col_blocks, width)
    quarters = to_all(head, "row", grid_rows)[:PANELS]
    gathered = to_all(quarters, "layer", x_size, x_groups)
    top = jnp.moveaxis(gathered, 0, 1).reshape(lead, col_blocks, width)

    mine = lax.dynamic_slice_in_dim(held, layer_here * share, share, 1)
    mine_first = mine[:, :, 0, :].reshape(row_blocks * share, width)
    swapped_in = jnp.concatenate([top[:, 0, :], mine_first], axis=0)
    swapped = lax.ppermute(swapped_in, "col", [(0, 1), (1, 0)])
    is_first = col_here == 0
    solved, weights = weigh(is_first.astype(jnp.int32)[None], swapped_in, swapped)

    half = lax.dynamic_slice_in_dim(weights, (col_here % 2) * width, width, 1)
    far = lax.ppermute(half, "col", [(0, 4), (1, 5)])
    half = jnp.where(col_here < 4, half, far)
    near = lax.ppermute(half, "col", [(0, 2), (1, 3), (4, 6), (5, 7)])
    half = jnp.where(col_here % 4 < 2, half, near)
    other = lax.ppermute(half, "col", [(i, i ^ 1) for i in range(grid_cols)])
    is_even = col_here % 2 == 0
    weights_here = jnp.concatenate(
        [jnp.where(is_even, half, other), jnp.where(is_even, other, half)], axis=1
    )
    update = product(weights_here, top.reshape(lead, col_blocks * width))
    trailing = mine - update.reshape(row_blocks, share, col_blocks, width)

    row_number = (jnp.arange(row_blocks, dtype=jnp.int32) * grid_rows + row_here)[:, None, None, None]
    col_number = (jnp.arange(col_blocks, dtype=jnp.int32) * grid_cols + col_here)[None, None, :, None]
    row_inside = (jnp.arange(share, dtype=jnp.int32) + layer_here * share)[None, :, None, None]
    col_inside = jnp.arange(width, dtype=jnp.int32)[None, None, None, :]
    panel = jnp.where(is_first, solved[:, :width], solved[:, width : 2 * width])
    panel = panel.reshape(row_blocks, share, 1, width)
    below = (row_number > col_number) | ((row_number == col_number) & (row_inside >= col_inside))
    panel = jnp.where(below, panel, 0.0)
    trailing = jnp.where(row_number < PANELS, 0.0, trailing)
    result = jnp.where(col_number < PANELS, panel, trailing)
    return result.reshape(row_blocks, 1, share, col_blocks, 1, width)


def solution(mesh):
    return jax.shard_map(
        local,
        mesh=mesh,
        in_specs=(P(None, "row", None, None, "col", None),),
        out_specs=P(None, "row", "layer", None, "col", None),
        check_vma=False,
    )
```

```python
import functools
import jax
import jax.numpy as jnp
from jax import lax
from jax.experimental import pallas as pl
from jax.experimental.pallas import tpu as pltpu
from jax.sharding import PartitionSpec as P

PANELS = 2
BLOCK = 128
STRIP = 64
HIGHEST = lax.Precision.HIGHEST


def product(left, right, dims=((1,), (0,))):
    return lax.dot_general(left, right, (dims, ((), ())), precision=HIGHEST, preferred_element_type=jnp.float32)

def spread_lane(part, lane, sublane):
    return jnp.where(sublane < 8, jnp.broadcast_to(part[:, lane : lane + 1], (8, 128)), 0.0)


def eliminate(groups, first_lane, work):
    count = len(groups)
    sublane = lax.broadcasted_iota(jnp.int32, (8, 128), 0)
    lane_id = lax.broadcasted_iota(jnp.int32, (8, 128), 1)
    parts = list(groups)
    def spread(i, lane, guard):
        if guard:
            return [spread_lane(parts[i], lane + s, sublane) for s in range(8)]
        return [jnp.broadcast_to(parts[i][:, lane + s : lane + s + 1], (8, 128)) for s in range(8)]
    current = spread(0, first_lane, True)
    for g in range(count):
        lane = first_lane + 8 * g
        more = g + 1 < count
        heads = [current + (spread(g, lane + 8, True) if more else [])]
        if more:
            heads.append(spread(g + 1, lane, False) + spread(g + 1, lane + 8, True))
        for i in range(g + 2, count):
            heads.append(spread(i, lane, False))
        inside = (lane_id >= lane) & (lane_id < lane + 8)
        unit = (lane_id - lane == sublane).astype(jnp.float32)
        for i in range(g, count):
            parts[i] = jnp.where(inside, unit if i == g else 0.0, parts[i])
        scale = None
        for s in range(8):
            below = jnp.where(sublane > s, heads[0][s], 0.0)
            head_rows = [
                jnp.broadcast_to(head[s : s + 1, :], (8, 128)) for head in heads[0][s + 1 :]
            ]
            root = lax.rsqrt(jnp.broadcast_to(heads[0][s][s : s + 1, :], (8, 128)))
            inverse = root * root
            scale = root if s == 0 else jnp.where(sublane == s, root, scale)
            row = jnp.broadcast_to(parts[g][s : s + 1, :], (8, 128))
            if s < 7:
                heads[0][s + 1] = heads[0][s + 1] - (below * head_rows[0]) * inverse
            for i in range(g, count):
                if i == g and s == 7:
                    continue
                factor = (below if i == g else heads[i - g][s]) * inverse
                parts[i] = parts[i] - factor * row
                for p in range(s + 1, len(heads[i - g])):
                    if i > g or p > s + 1:
                        heads[i - g][p] = heads[i - g][p] - factor * head_rows[p - s - 1]
        parts[g] = parts[g] * scale
        if more:
            current = heads[1][8:]
        work()
    return jnp.concatenate(parts, axis=0)


def factor_kernel(
    first_ref, mine_ref, other_ref, panel_ref, half_ref, v_ref, x_ref, w_ref, p_ref, e_ref, block_ref
):
    size = w_ref.shape[0]
    half = size // 2
    count = size // BLOCK
    first = first_ref[0] == 1
    def left(rows):
        return jnp.where(first, mine_ref[rows, :], other_ref[rows, :])
    def right(rows):
        return jnp.where(first, other_ref[rows, :], mine_ref[rows, :])
    w_ref[:half, :half] = left(slice(0, half))
    w_ref[:, half:] = right(slice(0, size))
    p_ref[:half, :] = left(slice(size, None)).T
    p_ref[half:, :] = right(slice(size, None)).T
    row_id = lax.broadcasted_iota(jnp.int32, (BLOCK, BLOCK), 0)
    col_id = lax.broadcasted_iota(jnp.int32, (BLOCK, BLOCK), 1)
    at = [slice(k * BLOCK, (k + 1) * BLOCK) for k in range(count)]
    pending = []
    for k in range(count):
        slots = 2 * STRIP // 8
        done_slots = [0]
        per = -(-len(pending) // (slots - 2)) if pending else 0
        def work():
            done_slots[0] += 1
            for _ in range(per):
                if pending:
                    pending.pop(0)()
        block_ref[...] = w_ref[at[k], at[k]]
        for begin in range(0, BLOCK, STRIP):
            end = begin + STRIP
            groups = [block_ref[begin + 8 * i : begin + 8 * i + 8, :] for i in range(STRIP // 8)]
            done = eliminate(groups, begin, work)
            rows, lanes = row_id[begin:end], col_id[begin:end]
            block_ref[begin:end, :] = jnp.where(lanes <= rows, done, 0.0)
            if end < BLOCK:
                done = jnp.where((lanes <= rows) | (lanes >= end), done, 0.0)
                rest = block_ref[end:, :]
                rest = jnp.where((col_id[end:] >= begin) & (col_id[end:] < end), 0.0, rest)
                block_ref[end:, :] = rest - product(done.T[end:], done)
        while pending:
            pending.pop(0)()
        e_ref[at[k], at[k]] = block_ref[...]
        if k < count - 1:
            inverse = block_ref[...]
            upper = product(inverse, w_ref[at[k], at[k + 1]])
            w_ref[at[k], at[k + 1]] = upper
            w_ref[at[k + 1], at[k + 1]] -= product(upper.T, upper)
            def panel(k=k, j=0):
                w_ref[at[k], at[j]] = product(e_ref[at[k], at[k]], w_ref[at[k], at[j]])
            def panel_p(k=k):
                p_ref[at[k], :] = product(e_ref[at[k], at[k]], p_ref[at[k], :])
            def panel_e(k=k):
                e_ref[at[k], : k * BLOCK] = product(e_ref[at[k], at[k]], e_ref[at[k], : k * BLOCK])
            def trail(k=k, i=0, j=0):
                w_ref[at[i], at[j]] -= product(w_ref[at[k], at[i]].T, w_ref[at[k], at[j]])
            def trail_p(k=k, i=0):
                p_ref[at[i], :] -= product(w_ref[at[k], at[i]].T, p_ref[at[k], :])
            def trail_e(k=k, i=0):
                lower = w_ref[at[k], at[i]].T
                e_ref[at[i], at[k]] = -product(lower, e_ref[at[k], at[k]])
                if k > 0:
                    e_ref[at[i], : k * BLOCK] -= product(lower, e_ref[at[k], : k * BLOCK])
            def output(k=k):
                solved = p_ref[at[k], :].T
                v_ref[:, at[k]] = solved
                x_ref[:, at[k]] = product(solved, e_ref[at[k], at[k]])
                if k > 0:
                    x_ref[:, : k * BLOCK] += product(solved, e_ref[at[k], : k * BLOCK])
            bind = functools.partial
            for j in range(k + 2, count):
                pending.append(bind(panel, j=j))
            pending.append(bind(panel_p))
            for i in range(k + 1, count):
                for j in range(i, count):
                    if j > k + 1:
                        pending.append(bind(trail, i=i, j=j))
                pending.append(bind(trail_p, i=i))
            if k > 0:
                pending.append(bind(panel_e))
            for i in range(k + 1, count):
                pending.append(bind(trail_e, i=i))
            pending.append(bind(output))
    last = at[count - 1]
    inverse = block_ref[...]
    solved = product(p_ref[last, :], inverse, ((0,), (1,)))
    v_ref[:, last] = solved
    weights = product(solved, inverse)
    x_ref[:, last] = weights
    x_ref[:, : size - BLOCK] += product(weights, e_ref[last, : size - BLOCK])
    panel_ref[...] = jnp.where(first, v_ref[:, :half], v_ref[:, half:])
    half_ref[...] = jnp.where(first, x_ref[:, :half], x_ref[:, half:])

def weigh(first, mine, other):
    size = 2 * mine.shape[1]
    share = mine.shape[0] - size
    shape = jax.ShapeDtypeStruct((share, size // 2), jnp.float32)
    whole = pl.BlockSpec(memory_space=pltpu.VMEM)
    return pl.pallas_call(
        factor_kernel,
        out_shape=[shape, shape],
        in_specs=[pl.BlockSpec(memory_space=pltpu.SMEM), whole, whole],
        out_specs=[whole, whole],
        scratch_shapes=[
            pltpu.VMEM((share, size), jnp.float32),
            pltpu.VMEM((share, size), jnp.float32),
            pltpu.VMEM((size, size), jnp.float32),
            pltpu.VMEM((size, share), jnp.float32),
            pltpu.VMEM((size, size), jnp.float32),
            pltpu.VMEM((BLOCK, BLOCK), jnp.float32),
        ],
        name="factor",
    )(first, mine, other)


def to_all(piece, axis, peers, groups=None):
    copies = jnp.broadcast_to(piece[None], (peers, *piece.shape))
    return lax.all_to_all(copies, axis, 0, 0, axis_index_groups=groups)


def local(schur_window):
    row_blocks, _, width, col_blocks, _, _ = schur_window.shape
    held = schur_window.reshape(row_blocks, width, col_blocks, width)
    layers = lax.axis_size("layer")
    grid_rows = lax.axis_size("row")
    grid_cols = lax.axis_size("col")
    layer_here = lax.axis_index("layer")
    row_here = lax.axis_index("row")
    col_here = lax.axis_index("col")
    x_size = layers // 2
    x_groups = [[x * 2 + z for x in range(x_size)] for z in range(2)]
    share = width // layers
    quarter = width // x_size
    lead = PANELS * width

    head = lax.dynamic_slice(
        schur_window,
        (0, 0, (layer_here // 2) * quarter, 0, 0, 0),
        (1, 1, quarter, col_blocks, 1, width),
    ).reshape(quarter, col_blocks, width)
    def collect(part, name):
        with jax.named_scope(name + "_row"):
            quarters = to_all(part, "row", grid_rows)[:PANELS]
        with jax.named_scope(name + "_x"):
            gathered = to_all(quarters, "layer", x_size, x_groups)
        return jnp.moveaxis(gathered, 0, 1).reshape(lead, -1)

    lead_part = collect(head[:, 0, :], "lead")
    rest_part = collect(head[:, 1:, :].reshape(quarter, (col_blocks - 1) * width), "rest")
    mine = lax.dynamic_slice_in_dim(held, layer_here * share, share, 1)
    mine_first = mine[:, :, 0, :].reshape(row_blocks * share, width)
    swapped_in = jnp.concatenate([lead_part, mine_first], axis=0)
    swapped = lax.ppermute(swapped_in, "col", [(0, 1), (1, 0)])
    is_first = col_here == 0
    with jax.named_scope("inverse"):
        panel, half = weigh(is_first.astype(jnp.int32)[None], swapped_in, swapped)
    far = lax.ppermute(half, "col", [(0, 4), (1, 5)])
    half = jnp.where(col_here < 4, half, far)
    near = lax.ppermute(half, "col", [(0, 2), (1, 3), (4, 6), (5, 7)])
    half = jnp.where(col_here % 4 < 2, half, near)
    other = lax.ppermute(half, "col", [(i, i ^ 1) for i in range(grid_cols)])
    is_even = col_here % 2 == 0
    weights_here = jnp.concatenate(
        [jnp.where(is_even, half, other), jnp.where(is_even, other, half)], axis=1
    )
    update = product(weights_here, jnp.concatenate([lead_part, rest_part], axis=1))
    trailing = mine - update.reshape(row_blocks, share, col_blocks, width)

    row_number = (jnp.arange(row_blocks, dtype=jnp.int32) * grid_rows + row_here)[:, None, None, None]
    col_number = (jnp.arange(col_blocks, dtype=jnp.int32) * grid_cols + col_here)[None, None, :, None]
    row_inside = (jnp.arange(share, dtype=jnp.int32) + layer_here * share)[None, :, None, None]
    col_inside = jnp.arange(width, dtype=jnp.int32)[None, None, None, :]
    panel = panel.reshape(row_blocks, share, 1, width)
    below = (row_number > col_number) | ((row_number == col_number) & (row_inside >= col_inside))
    panel = jnp.where(below, panel, 0.0)
    trailing = jnp.where(row_number < PANELS, 0.0, trailing)
    result = jnp.where(col_number < PANELS, panel, trailing)
    return result.reshape(row_blocks, 1, share, col_blocks, 1, width)


def solution(mesh):
    return jax.shard_map(
        local,
        mesh=mesh,
        in_specs=(P(None, "row", None, None, "col", None),),
        out_specs=P(None, "row", "layer", None, "col", None),
        check_vma=False,
    )
```

```python
import functools
import jax
import jax.numpy as jnp
from jax import lax
from jax.experimental import pallas as pl
from jax.experimental.pallas import tpu as pltpu
from jax.sharding import PartitionSpec as P

PANELS = 2
BLOCK = 128
STRIP = 64
HIGHEST = lax.Precision.HIGHEST


def product(left, right, dims=((1,), (0,))):
    return lax.dot_general(left, right, (dims, ((), ())), precision=HIGHEST, preferred_element_type=jnp.float32)

def spread_lane(part, lane, sublane):
    return jnp.where(sublane < 8, jnp.broadcast_to(part[:, lane : lane + 1], (8, 128)), 0.0)


def eliminate(groups, first_lane, work):
    count = len(groups)
    sublane = lax.broadcasted_iota(jnp.int32, (8, 128), 0)
    lane_id = lax.broadcasted_iota(jnp.int32, (8, 128), 1)
    parts = list(groups)
    def spread(i, lane, guard):
        if guard:
            return [spread_lane(parts[i], lane + s, sublane) for s in range(8)]
        return [jnp.broadcast_to(parts[i][:, lane + s : lane + s + 1], (8, 128)) for s in range(8)]
    current = spread(0, first_lane, True)
    for g in range(count):
        lane = first_lane + 8 * g
        more = g + 1 < count
        heads = [current + (spread(g, lane + 8, True) if more else [])]
        if more:
            heads.append(spread(g + 1, lane, False) + spread(g + 1, lane + 8, True))
        for i in range(g + 2, count):
            heads.append(spread(i, lane, False))
        inside = (lane_id >= lane) & (lane_id < lane + 8)
        unit = (lane_id - lane == sublane).astype(jnp.float32)
        for i in range(g, count):
            parts[i] = jnp.where(inside, unit if i == g else 0.0, parts[i])
        scale = None
        for s in range(8):
            below = jnp.where(sublane > s, heads[0][s], 0.0)
            head_rows = [
                jnp.broadcast_to(head[s : s + 1, :], (8, 128)) for head in heads[0][s + 1 :]
            ]
            root = lax.rsqrt(jnp.broadcast_to(heads[0][s][s : s + 1, :], (8, 128)))
            inverse = root * root
            scale = root if s == 0 else jnp.where(sublane == s, root, scale)
            row = jnp.broadcast_to(parts[g][s : s + 1, :], (8, 128))
            if s < 7:
                heads[0][s + 1] = heads[0][s + 1] - (below * head_rows[0]) * inverse
            for i in range(g, count):
                if i == g and s == 7:
                    continue
                factor = (below if i == g else heads[i - g][s]) * inverse
                parts[i] = parts[i] - factor * row
                for p in range(s + 1, len(heads[i - g])):
                    if i > g or p > s + 1:
                        heads[i - g][p] = heads[i - g][p] - factor * head_rows[p - s - 1]
        parts[g] = parts[g] * scale
        if more:
            current = heads[1][8:]
        work()
    return jnp.concatenate(parts, axis=0)


def factor_kernel(
    first_ref, mine_ref, other_ref, panel_ref, half_ref, v_ref, x_ref, w_ref, p_ref, e_ref, block_ref
):
    size = w_ref.shape[0]
    half = size // 2
    count = size // BLOCK
    first = first_ref[0] == 1
    def left(rows):
        return jnp.where(first, mine_ref[rows, :], other_ref[rows, :])
    def right(rows):
        return jnp.where(first, other_ref[rows, :], mine_ref[rows, :])
    w_ref[:half, :half] = left(slice(0, half))
    w_ref[:, half:] = right(slice(0, size))
    p_ref[:half, :] = left(slice(size, None)).T
    p_ref[half:, :] = right(slice(size, None)).T
    row_id = lax.broadcasted_iota(jnp.int32, (BLOCK, BLOCK), 0)
    col_id = lax.broadcasted_iota(jnp.int32, (BLOCK, BLOCK), 1)
    at = [slice(k * BLOCK, (k + 1) * BLOCK) for k in range(count)]
    pending = []
    for k in range(count):
        slots = 2 * STRIP // 8
        done_slots = [0]
        per = -(-len(pending) // (slots - 2)) if pending else 0
        def work():
            done_slots[0] += 1
            for _ in range(per):
                if pending:
                    pending.pop(0)()
        block_ref[...] = w_ref[at[k], at[k]]
        for begin in range(0, BLOCK, STRIP):
            end = begin + STRIP
            groups = [block_ref[begin + 8 * i : begin + 8 * i + 8, :] for i in range(STRIP // 8)]
            done = eliminate(groups, begin, work)
            rows, lanes = row_id[begin:end], col_id[begin:end]
            block_ref[begin:end, :] = jnp.where(lanes <= rows, done, 0.0)
            if end < BLOCK:
                done = jnp.where((lanes <= rows) | (lanes >= end), done, 0.0)
                rest = block_ref[end:, :]
                rest = jnp.where((col_id[end:] >= begin) & (col_id[end:] < end), 0.0, rest)
                block_ref[end:, :] = rest - product(done.T[end:], done)
        while pending:
            pending.pop(0)()
        e_ref[at[k], at[k]] = block_ref[...]
        if k < count - 1:
            inverse = block_ref[...]
            upper = product(inverse, w_ref[at[k], at[k + 1]])
            w_ref[at[k], at[k + 1]] = upper
            w_ref[at[k + 1], at[k + 1]] -= product(upper.T, upper)
            def panel(k=k, j=0):
                w_ref[at[k], at[j]] = product(e_ref[at[k], at[k]], w_ref[at[k], at[j]])
            def panel_p(k=k):
                p_ref[at[k], :] = product(e_ref[at[k], at[k]], p_ref[at[k], :])
            def panel_e(k=k):
                e_ref[at[k], : k * BLOCK] = product(e_ref[at[k], at[k]], e_ref[at[k], : k * BLOCK])
            def trail(k=k, i=0, j=0):
                w_ref[at[i], at[j]] -= product(w_ref[at[k], at[i]].T, w_ref[at[k], at[j]])
            def trail_p(k=k, i=0):
                p_ref[at[i], :] -= product(w_ref[at[k], at[i]].T, p_ref[at[k], :])
            def trail_e(k=k, i=0):
                lower = w_ref[at[k], at[i]].T
                e_ref[at[i], at[k]] = -product(lower, e_ref[at[k], at[k]])
                if k > 0:
                    e_ref[at[i], : k * BLOCK] -= product(lower, e_ref[at[k], : k * BLOCK])
            def output(k=k):
                solved = p_ref[at[k], :].T
                v_ref[:, at[k]] = solved
                x_ref[:, at[k]] = product(solved, e_ref[at[k], at[k]])
                if k > 0:
                    x_ref[:, : k * BLOCK] += product(solved, e_ref[at[k], : k * BLOCK])
            bind = functools.partial
            for j in range(k + 2, count):
                pending.append(bind(panel, j=j))
            pending.append(bind(panel_p))
            for i in range(k + 1, count):
                for j in range(i, count):
                    if j > k + 1:
                        pending.append(bind(trail, i=i, j=j))
                pending.append(bind(trail_p, i=i))
            if k > 0:
                pending.append(bind(panel_e))
            for i in range(k + 1, count):
                pending.append(bind(trail_e, i=i))
            pending.append(bind(output))
    last = at[count - 1]
    inverse = block_ref[...]
    solved = product(p_ref[last, :], inverse, ((0,), (1,)))
    v_ref[:, last] = solved
    weights = product(solved, inverse)
    x_ref[:, last] = weights
    x_ref[:, : size - BLOCK] += product(weights, e_ref[last, : size - BLOCK])
    panel_ref[...] = jnp.where(first, v_ref[:, :half], v_ref[:, half:])
    half_ref[...] = jnp.where(first, x_ref[:, :half], x_ref[:, half:])

def weigh(first, mine, other):
    size = 2 * mine.shape[1]
    share = mine.shape[0] - size
    shape = jax.ShapeDtypeStruct((share, size // 2), jnp.float32)
    whole = pl.BlockSpec(memory_space=pltpu.VMEM)
    return pl.pallas_call(
        factor_kernel,
        out_shape=[shape, shape],
        in_specs=[pl.BlockSpec(memory_space=pltpu.SMEM), whole, whole],
        out_specs=[whole, whole],
        scratch_shapes=[
            pltpu.VMEM((share, size), jnp.float32),
            pltpu.VMEM((share, size), jnp.float32),
            pltpu.VMEM((size, size), jnp.float32),
            pltpu.VMEM((size, share), jnp.float32),
            pltpu.VMEM((size, size), jnp.float32),
            pltpu.VMEM((BLOCK, BLOCK), jnp.float32),
        ],
        compiler_params=pltpu.CompilerParams(vmem_limit_bytes=16 << 20),
        name="factor",
    )(first, mine, other)


def to_all(piece, axis, peers, groups=None):
    copies = jnp.broadcast_to(piece[None], (peers, *piece.shape))
    return lax.all_to_all(copies, axis, 0, 0, axis_index_groups=groups)


def local(schur_window):
    row_blocks, _, width, col_blocks, _, _ = schur_window.shape
    held = schur_window.reshape(row_blocks, width, col_blocks, width)
    layers = lax.axis_size("layer")
    grid_rows = lax.axis_size("row")
    grid_cols = lax.axis_size("col")
    layer_here = lax.axis_index("layer")
    row_here = lax.axis_index("row")
    col_here = lax.axis_index("col")
    x_size = layers // 2
    x_groups = [[x * 2 + z for x in range(x_size)] for z in range(2)]
    share = width // layers
    quarter = width // x_size
    lead = PANELS * width

    head = lax.dynamic_slice(
        schur_window,
        (0, 0, (layer_here // 2) * quarter, 0, 0, 0),
        (1, 1, quarter, col_blocks, 1, width),
    ).reshape(quarter, col_blocks, width)
    def collect(part, name):
        with jax.named_scope(name + "_row"):
            quarters = to_all(part, "row", grid_rows)[:PANELS]
        with jax.named_scope(name + "_x"):
            gathered = to_all(quarters, "layer", x_size, x_groups)
        return jnp.moveaxis(gathered, 0, 1).reshape(lead, -1)

    lead_part = collect(head[:, 0, :], "lead")
    rest_part = collect(head[:, 1:, :].reshape(quarter, (col_blocks - 1) * width), "rest")
    mine = lax.dynamic_slice_in_dim(held, layer_here * share, share, 1)
    mine_first = mine[:, :, 0, :].reshape(row_blocks * share, width)
    swapped_in = jnp.concatenate([lead_part, mine_first], axis=0)
    swapped = lax.ppermute(swapped_in, "col", [(0, 1), (1, 0)])
    is_first = col_here == 0
    with jax.named_scope("inverse"):
        panel, half = weigh(is_first.astype(jnp.int32)[None], swapped_in, swapped)
    far = lax.ppermute(half, "col", [(0, 4), (1, 5)])
    half = jnp.where(col_here < 4, half, far)
    near = lax.ppermute(half, "col", [(0, 2), (1, 3), (4, 6), (5, 7)])
    half = jnp.where(col_here % 4 < 2, half, near)
    other = lax.ppermute(half, "col", [(i, i ^ 1) for i in range(grid_cols)])
    is_even = col_here % 2 == 0
    weights_here = jnp.concatenate(
        [jnp.where(is_even, half, other), jnp.where(is_even, other, half)], axis=1
    )
    update = product(weights_here, jnp.concatenate([lead_part, rest_part], axis=1))
    trailing = mine - update.reshape(row_blocks, share, col_blocks, width)

    row_number = (jnp.arange(row_blocks, dtype=jnp.int32) * grid_rows + row_here)[:, None, None, None]
    col_number = (jnp.arange(col_blocks, dtype=jnp.int32) * grid_cols + col_here)[None, None, :, None]
    row_inside = (jnp.arange(share, dtype=jnp.int32) + layer_here * share)[None, :, None, None]
    col_inside = jnp.arange(width, dtype=jnp.int32)[None, None, None, :]
    panel = panel.reshape(row_blocks, share, 1, width)
    below = (row_number > col_number) | ((row_number == col_number) & (row_inside >= col_inside))
    panel = jnp.where(below, panel, 0.0)
    trailing = jnp.where(row_number < PANELS, 0.0, trailing)
    result = jnp.where(col_number < PANELS, panel, trailing)
    return result.reshape(row_blocks, 1, share, col_blocks, 1, width)


def solution(mesh):
    return jax.shard_map(
        local,
        mesh=mesh,
        in_specs=(P(None, "row", None, None, "col", None),),
        out_specs=P(None, "row", "layer", None, "col", None),
        check_vma=False,
    )
```

```python
import functools
import jax
import jax.numpy as jnp
from jax import lax
from jax.experimental import pallas as pl
from jax.experimental.pallas import tpu as pltpu
from jax.sharding import PartitionSpec as P

PANELS = 2
BLOCK = 128
STRIP = 64
HIGHEST = lax.Precision.HIGHEST


def product(left, right, dims=((1,), (0,))):
    return lax.dot_general(left, right, (dims, ((), ())), precision=HIGHEST, preferred_element_type=jnp.float32)


def spread_lane(part, lane, sublane):
    return jnp.where(sublane < 8, jnp.broadcast_to(part[:, lane : lane + 1], (8, 128)), 0.0)


def eliminate(groups, first_lane, work):
    count = len(groups)
    sublane = lax.broadcasted_iota(jnp.int32, (8, 128), 0)
    lane_id = lax.broadcasted_iota(jnp.int32, (8, 128), 1)
    parts = list(groups)
    def spread(i, lane, guard):
        if guard:
            return [spread_lane(parts[i], lane + s, sublane) for s in range(8)]
        return [jnp.broadcast_to(parts[i][:, lane + s : lane + s + 1], (8, 128)) for s in range(8)]
    current = spread(0, first_lane, True)
    for g in range(count):
        lane = first_lane + 8 * g
        more = g + 1 < count
        heads = [current + (spread(g, lane + 8, True) if more else [])]
        if more:
            heads.append(spread(g + 1, lane, False) + spread(g + 1, lane + 8, True))
        for i in range(g + 2, count):
            heads.append(spread(i, lane, False))
        inside = (lane_id >= lane) & (lane_id < lane + 8)
        unit = (lane_id - lane == sublane).astype(jnp.float32)
        for i in range(g, count):
            parts[i] = jnp.where(inside, unit if i == g else 0.0, parts[i])
        scale = None
        for s in range(8):
            below = jnp.where(sublane > s, heads[0][s], 0.0)
            head_rows = [
                jnp.broadcast_to(head[s : s + 1, :], (8, 128)) for head in heads[0][s + 1 :]
            ]
            root = lax.rsqrt(jnp.broadcast_to(heads[0][s][s : s + 1, :], (8, 128)))
            inverse = root * root
            scale = root if s == 0 else jnp.where(sublane == s, root, scale)
            row = jnp.broadcast_to(parts[g][s : s + 1, :], (8, 128))
            if s < 7:
                heads[0][s + 1] = heads[0][s + 1] - (below * head_rows[0]) * inverse
            for i in range(g, count):
                if i == g and s == 7:
                    continue
                factor = (below if i == g else heads[i - g][s]) * inverse
                parts[i] = parts[i] - factor * row
                for p in range(s + 1, len(heads[i - g])):
                    if i > g or p > s + 1:
                        heads[i - g][p] = heads[i - g][p] - factor * head_rows[p - s - 1]
        parts[g] = parts[g] * scale
        if more:
            current = heads[1][8:]
        work()
    return jnp.concatenate(parts, axis=0)


def factor_body(
    first, mine_ref, other_ref, panel_ref, half_ref, v_ref, x_ref, w_ref, p_ref, e_ref, block_ref
):
    size = w_ref.shape[0]
    half = size // 2
    count = size // BLOCK
    def left(rows):
        return jnp.where(first, mine_ref[rows, :], other_ref[rows, :])
    def right(rows):
        return jnp.where(first, other_ref[rows, :], mine_ref[rows, :])
    w_ref[:half, :half] = left(slice(0, half))
    w_ref[:, half:] = right(slice(0, size))
    p_ref[:half, :] = left(slice(size, None)).T
    p_ref[half:, :] = right(slice(size, None)).T
    row_id = lax.broadcasted_iota(jnp.int32, (BLOCK, BLOCK), 0)
    col_id = lax.broadcasted_iota(jnp.int32, (BLOCK, BLOCK), 1)
    at = [slice(k * BLOCK, (k + 1) * BLOCK) for k in range(count)]
    pending = []
    for k in range(count):
        slots = 2 * STRIP // 8
        per = -(-len(pending) // (slots - 2)) if pending else 0
        def work():
            for _ in range(per):
                if pending:
                    pending.pop(0)()
        block_ref[...] = w_ref[at[k], at[k]]
        for begin in range(0, BLOCK, STRIP):
            end = begin + STRIP
            groups = [block_ref[begin + 8 * i : begin + 8 * i + 8, :] for i in range(STRIP // 8)]
            done = eliminate(groups, begin, work)
            rows, lanes = row_id[begin:end], col_id[begin:end]
            block_ref[begin:end, :] = jnp.where(lanes <= rows, done, 0.0)
            if end < BLOCK:
                done = jnp.where((lanes <= rows) | (lanes >= end), done, 0.0)
                rest = block_ref[end:, :]
                rest = jnp.where((col_id[end:] >= begin) & (col_id[end:] < end), 0.0, rest)
                block_ref[end:, :] = rest - product(done.T[end:], done)
        while pending:
            pending.pop(0)()
        e_ref[at[k], at[k]] = block_ref[...]
        if k < count - 1:
            inverse = block_ref[...]
            upper = product(inverse, w_ref[at[k], at[k + 1]])
            w_ref[at[k], at[k + 1]] = upper
            w_ref[at[k + 1], at[k + 1]] -= product(upper.T, upper)
            def panel(k=k, j=0):
                w_ref[at[k], at[j]] = product(e_ref[at[k], at[k]], w_ref[at[k], at[j]])
            def panel_p(k=k):
                p_ref[at[k], :] = product(e_ref[at[k], at[k]], p_ref[at[k], :])
            def panel_e(k=k):
                e_ref[at[k], : k * BLOCK] = product(e_ref[at[k], at[k]], e_ref[at[k], : k * BLOCK])
            def trail(k=k, i=0, j=0):
                w_ref[at[i], at[j]] -= product(w_ref[at[k], at[i]].T, w_ref[at[k], at[j]])
            def trail_p(k=k, i=0):
                p_ref[at[i], :] -= product(w_ref[at[k], at[i]].T, p_ref[at[k], :])
            def trail_e(k=k, i=0):
                lower = w_ref[at[k], at[i]].T
                e_ref[at[i], at[k]] = -product(lower, e_ref[at[k], at[k]])
                if k > 0:
                    e_ref[at[i], : k * BLOCK] -= product(lower, e_ref[at[k], : k * BLOCK])
            def output(k=k):
                solved = p_ref[at[k], :].T
                v_ref[:, at[k]] = solved
                x_ref[:, at[k]] = product(solved, e_ref[at[k], at[k]])
                if k > 0:
                    x_ref[:, : k * BLOCK] += product(solved, e_ref[at[k], : k * BLOCK])
            bind = functools.partial
            for j in range(k + 2, count):
                pending.append(bind(panel, j=j))
            pending.append(panel_p)
            for i in range(k + 1, count):
                for j in range(i, count):
                    if j > k + 1:
                        pending.append(bind(trail, i=i, j=j))
                pending.append(bind(trail_p, i=i))
            if k > 0:
                pending.append(panel_e)
            for i in range(k + 1, count):
                pending.append(bind(trail_e, i=i))
            pending.append(output)
    last = at[count - 1]
    inverse = block_ref[...]
    solved = product(p_ref[last, :], inverse, ((0,), (1,)))
    v_ref[:, last] = solved
    weights = product(solved, inverse)
    x_ref[:, last] = weights
    x_ref[:, : size - BLOCK] += product(weights, e_ref[last, : size - BLOCK])
    panel_ref[...] = jnp.where(first, v_ref[:, :half], v_ref[:, half:])
    half_ref[...] = jnp.where(first, x_ref[:, :half], x_ref[:, half:])


def factor_kernel(position_ref, mine_ref, other_ref, panel_ref, half_ref, *scratch):
    position = position_ref[0]

    @pl.when(position < 2)
    def _():
        factor_body(position == 0, mine_ref, other_ref, panel_ref, half_ref, *scratch)

    @pl.when(position >= 2)
    def _():
        panel_ref[...] = jnp.zeros_like(panel_ref)
        half_ref[...] = jnp.zeros_like(half_ref)


def weigh(position, mine, other):
    size = 2 * mine.shape[1]
    share = mine.shape[0] - size
    shape = jax.ShapeDtypeStruct((share, size // 2), jnp.float32)
    whole = pl.BlockSpec(memory_space=pltpu.VMEM)
    return pl.pallas_call(
        factor_kernel,
        out_shape=[shape, shape],
        in_specs=[pl.BlockSpec(memory_space=pltpu.SMEM), whole, whole],
        out_specs=[whole, whole],
        scratch_shapes=[
            pltpu.VMEM((share, size), jnp.float32),
            pltpu.VMEM((share, size), jnp.float32),
            pltpu.VMEM((size, size), jnp.float32),
            pltpu.VMEM((size, share), jnp.float32),
            pltpu.VMEM((size, size), jnp.float32),
            pltpu.VMEM((BLOCK, BLOCK), jnp.float32),
        ],
        compiler_params=pltpu.CompilerParams(vmem_limit_bytes=16 << 20),
        name="factor",
    )(position, mine, other)


def to_all(piece, axis, peers, groups=None):
    copies = jnp.broadcast_to(piece[None], (peers, *piece.shape))
    return lax.all_to_all(copies, axis, 0, 0, axis_index_groups=groups)


def local(schur_window):
    row_blocks, _, width, col_blocks, _, _ = schur_window.shape
    held = schur_window.reshape(row_blocks, width, col_blocks, width)
    layers = lax.axis_size("layer")
    grid_rows = lax.axis_size("row")
    grid_cols = lax.axis_size("col")
    layer_here = lax.axis_index("layer")
    row_here = lax.axis_index("row")
    col_here = lax.axis_index("col")
    x_size = layers // 2
    x_groups = [[x * 2 + z for x in range(x_size)] for z in range(2)]
    share = width // layers
    quarter = width // x_size
    lead = PANELS * width

    head = lax.dynamic_slice(
        schur_window,
        (0, 0, (layer_here // 2) * quarter, 0, 0, 0),
        (1, 1, quarter, col_blocks, 1, width),
    ).reshape(quarter, col_blocks, width)
    def collect(part):
        quarters = to_all(part, "row", grid_rows)[:PANELS]
        gathered = to_all(quarters, "layer", x_size, x_groups)
        return jnp.moveaxis(gathered, 0, 1).reshape(lead, -1)

    lead_part = collect(head[:, 0, :])
    rest_part = collect(head[:, 1:, :].reshape(quarter, (col_blocks - 1) * width))
    mine = lax.dynamic_slice_in_dim(held, layer_here * share, share, 1)
    mine_first = mine[:, :, 0, :].reshape(row_blocks * share, width)
    swapped_in = jnp.concatenate([lead_part, mine_first], axis=0)
    swapped = lax.ppermute(swapped_in, "col", [(0, 1), (1, 0)])
    panel, half = weigh(col_here[None], swapped_in, swapped)
    far = lax.ppermute(half, "col", [(0, 4), (1, 5)])
    half = jnp.where(col_here < 4, half, far)
    near = lax.ppermute(half, "col", [(0, 2), (1, 3), (4, 6), (5, 7)])
    half = jnp.where(col_here % 4 < 2, half, near)
    other = lax.ppermute(half, "col", [(i, i ^ 1) for i in range(grid_cols)])
    is_even = col_here % 2 == 0
    weights_here = jnp.concatenate(
        [jnp.where(is_even, half, other), jnp.where(is_even, other, half)], axis=1
    )
    update = product(weights_here, jnp.concatenate([lead_part, rest_part], axis=1))
    trailing = mine - update.reshape(row_blocks, share, col_blocks, width)

    row_number = (jnp.arange(row_blocks, dtype=jnp.int32) * grid_rows + row_here)[:, None, None, None]
    col_number = (jnp.arange(col_blocks, dtype=jnp.int32) * grid_cols + col_here)[None, None, :, None]
    row_inside = (jnp.arange(share, dtype=jnp.int32) + layer_here * share)[None, :, None, None]
    col_inside = jnp.arange(width, dtype=jnp.int32)[None, None, None, :]
    panel = panel.reshape(row_blocks, share, 1, width)
    below = (row_number > col_number) | ((row_number == col_number) & (row_inside >= col_inside))
    panel = jnp.where(below, panel, 0.0)
    trailing = jnp.where(row_number < PANELS, 0.0, trailing)
    result = jnp.where(col_number < PANELS, panel, trailing)
    return result.reshape(row_blocks, 1, share, col_blocks, 1, width)


def solution(mesh):
    return jax.shard_map(
        local,
        mesh=mesh,
        in_specs=(P(None, "row", None, None, "col", None),),
        out_specs=P(None, "row", "layer", None, "col", None),
        check_vma=False,
    )
```

```python
import functools
import jax
import jax.numpy as jnp
from jax import lax
from jax.experimental import pallas as pl
from jax.experimental.pallas import tpu as pltpu
from jax.sharding import PartitionSpec as P

PANELS = 2
BLOCK = 128
STRIP = 64
HIGHEST = lax.Precision.HIGHEST


def product(left, right, dims=((1,), (0,))):
    return lax.dot_general(left, right, (dims, ((), ())), precision=HIGHEST, preferred_element_type=jnp.float32)


def spread_lane(part, lane, sublane):
    return jnp.where(sublane < 8, jnp.broadcast_to(part[:, lane : lane + 1], (8, 128)), 0.0)


def eliminate(groups, first_lane, work):
    count = len(groups)
    sublane = lax.broadcasted_iota(jnp.int32, (8, 128), 0)
    lane_id = lax.broadcasted_iota(jnp.int32, (8, 128), 1)
    parts = list(groups)
    def spread(i, lane, guard):
        if guard:
            return [spread_lane(parts[i], lane + s, sublane) for s in range(8)]
        return [jnp.broadcast_to(parts[i][:, lane + s : lane + s + 1], (8, 128)) for s in range(8)]
    current = spread(0, first_lane, True)
    for g in range(count):
        lane = first_lane + 8 * g
        more = g + 1 < count
        heads = [current + (spread(g, lane + 8, True) if more else [])]
        if more:
            heads.append(spread(g + 1, lane, False) + spread(g + 1, lane + 8, True))
        for i in range(g + 2, count):
            heads.append(spread(i, lane, False))
        inside = (lane_id >= lane) & (lane_id < lane + 8)
        unit = (lane_id - lane == sublane).astype(jnp.float32)
        for i in range(g, count):
            parts[i] = jnp.where(inside, unit if i == g else 0.0, parts[i])
        scale = None
        for s in range(8):
            below = jnp.where(sublane > s, heads[0][s], 0.0)
            head_rows = [
                jnp.broadcast_to(head[s : s + 1, :], (8, 128)) for head in heads[0][s + 1 :]
            ]
            root = lax.rsqrt(jnp.broadcast_to(heads[0][s][s : s + 1, :], (8, 128)))
            inverse = root * root
            scale = root if s == 0 else jnp.where(sublane == s, root, scale)
            row = jnp.broadcast_to(parts[g][s : s + 1, :], (8, 128))
            if s < 7:
                heads[0][s + 1] = heads[0][s + 1] - (below * head_rows[0]) * inverse
            for i in range(g, count):
                if i == g and s == 7:
                    continue
                factor = (below if i == g else heads[i - g][s]) * inverse
                parts[i] = parts[i] - factor * row
                for p in range(s + 1, len(heads[i - g])):
                    if i > g or p > s + 1:
                        heads[i - g][p] = heads[i - g][p] - factor * head_rows[p - s - 1]
        parts[g] = parts[g] * scale
        if more:
            current = heads[1][8:]
        work()
    return jnp.concatenate(parts, axis=0)


def factor_body(
    first, mine_ref, other_ref, panel_ref, half_ref, v_ref, x_ref, w_ref, p_ref, e_ref, block_ref
):
    size = w_ref.shape[0]
    half = size // 2
    count = size // BLOCK
    def left(rows):
        return jnp.where(first, mine_ref[rows, :], other_ref[rows, :])
    def right(rows):
        return jnp.where(first, other_ref[rows, :], mine_ref[rows, :])
    w_ref[:half, :half] = left(slice(0, half))
    w_ref[:, half:] = right(slice(0, size))
    p_ref[:half, :] = left(slice(size, None)).T
    p_ref[half:, :] = right(slice(size, None)).T
    row_id = lax.broadcasted_iota(jnp.int32, (BLOCK, BLOCK), 0)
    col_id = lax.broadcasted_iota(jnp.int32, (BLOCK, BLOCK), 1)
    at = [slice(k * BLOCK, (k + 1) * BLOCK) for k in range(count)]
    pending = []
    for k in range(count):
        slots = 2 * STRIP // 8
        per = -(-len(pending) // (slots - 2)) if pending else 0
        def work():
            for _ in range(per):
                if pending:
                    pending.pop(0)()
        block_ref[...] = w_ref[at[k], at[k]]
        for begin in range(0, BLOCK, STRIP):
            end = begin + STRIP
            groups = [block_ref[begin + 8 * i : begin + 8 * i + 8, :] for i in range(STRIP // 8)]
            done = eliminate(groups, begin, work)
            rows, lanes = row_id[begin:end], col_id[begin:end]
            block_ref[begin:end, :] = jnp.where(lanes <= rows, done, 0.0)
            if end < BLOCK:
                done = jnp.where((lanes <= rows) | (lanes >= end), done, 0.0)
                rest = block_ref[end:, :]
                rest = jnp.where((col_id[end:] >= begin) & (col_id[end:] < end), 0.0, rest)
                block_ref[end:, :] = rest - product(done.T[end:], done)
        while pending:
            pending.pop(0)()
        e_ref[at[k], at[k]] = block_ref[...]
        if k < count - 1:
            inverse = block_ref[...]
            upper = product(inverse, w_ref[at[k], at[k + 1]])
            w_ref[at[k], at[k + 1]] = upper
            w_ref[at[k + 1], at[k + 1]] -= product(upper.T, upper)
            def panel(k=k, j=0):
                w_ref[at[k], at[j]] = product(e_ref[at[k], at[k]], w_ref[at[k], at[j]])
            def panel_p(k=k):
                p_ref[at[k], :] = product(e_ref[at[k], at[k]], p_ref[at[k], :])
            def panel_e(k=k):
                e_ref[at[k], : k * BLOCK] = product(e_ref[at[k], at[k]], e_ref[at[k], : k * BLOCK])
            def trail(k=k, i=0, j=0):
                w_ref[at[i], at[j]] -= product(w_ref[at[k], at[i]].T, w_ref[at[k], at[j]])
            def trail_p(k=k, i=0):
                p_ref[at[i], :] -= product(w_ref[at[k], at[i]].T, p_ref[at[k], :])
            def trail_e(k=k, i=0):
                lower = w_ref[at[k], at[i]].T
                e_ref[at[i], at[k]] = -product(lower, e_ref[at[k], at[k]])
                if k > 0:
                    e_ref[at[i], : k * BLOCK] -= product(lower, e_ref[at[k], : k * BLOCK])
            def output(k=k):
                solved = p_ref[at[k], :].T
                v_ref[:, at[k]] = solved
                x_ref[:, at[k]] = product(solved, e_ref[at[k], at[k]])
                if k > 0:
                    x_ref[:, : k * BLOCK] += product(solved, e_ref[at[k], : k * BLOCK])
            bind = functools.partial
            for j in range(k + 2, count):
                pending.append(bind(panel, j=j))
            pending.append(panel_p)
            for i in range(k + 1, count):
                for j in range(i, count):
                    if j > k + 1:
                        pending.append(bind(trail, i=i, j=j))
                pending.append(bind(trail_p, i=i))
            if k > 0:
                pending.append(panel_e)
            for i in range(k + 1, count):
                pending.append(bind(trail_e, i=i))
            pending.append(output)
    last = at[count - 1]
    inverse = block_ref[...]
    solved = product(p_ref[last, :], inverse, ((0,), (1,)))
    v_ref[:, last] = solved
    weights = product(solved, inverse)
    x_ref[:, last] = weights
    x_ref[:, : size - BLOCK] += product(weights, e_ref[last, : size - BLOCK])
    panel_ref[...] = jnp.where(first, v_ref[:, :half], v_ref[:, half:])
    half_ref[...] = jnp.where(first, x_ref[:, :half], x_ref[:, half:])


def factor_kernel(position_ref, mine_ref, other_ref, panel_ref, half_ref, *scratch):
    position = position_ref[0]

    @pl.when(position < 2)
    def _():
        factor_body(position == 0, mine_ref, other_ref, panel_ref, half_ref, *scratch)

    @pl.when(position >= 2)
    def _():
        panel_ref[...] = jnp.zeros_like(panel_ref)
        half_ref[...] = jnp.zeros_like(half_ref)


def weigh(position, mine, other):
    size = 2 * mine.shape[1]
    share = mine.shape[0] - size
    shape = jax.ShapeDtypeStruct((share, size // 2), jnp.float32)
    whole = pl.BlockSpec(memory_space=pltpu.VMEM)
    return pl.pallas_call(
        factor_kernel,
        out_shape=[shape, shape],
        in_specs=[pl.BlockSpec(memory_space=pltpu.SMEM), whole, whole],
        out_specs=[whole, whole],
        scratch_shapes=[
            pltpu.VMEM((share, size), jnp.float32),
            pltpu.VMEM((share, size), jnp.float32),
            pltpu.VMEM((size, size), jnp.float32),
            pltpu.VMEM((size, share), jnp.float32),
            pltpu.VMEM((size, size), jnp.float32),
            pltpu.VMEM((BLOCK, BLOCK), jnp.float32),
        ],
        compiler_params=pltpu.CompilerParams(vmem_limit_bytes=16 << 20),
        name="factor",
    )(position, mine, other)


def copies_kernel(start_ref, window_ref, lead_ref, rest_ref, part_ref, arrived):
    rows = part_ref.shape[0]
    begin = pl.multiple_of(start_ref[0] * rows, rows)
    copy = pltpu.make_async_copy(window_ref.at[0, 0, pl.ds(begin, rows)], part_ref, arrived)
    copy.start()
    copy.wait()
    for slot, out_ref in enumerate((lead_ref, rest_ref)):
        part = part_ref[:, slot, 0, :]
        for peer in range(out_ref.shape[0]):
            out_ref[peer] = part


def copies(start, window, peers, rows):
    slots, width = window.shape[3], window.shape[5]
    shape = jax.ShapeDtypeStruct((peers, rows, width), jnp.float32)
    whole = pl.BlockSpec(memory_space=pltpu.VMEM)
    return pl.pallas_call(
        copies_kernel,
        out_shape=[shape, shape],
        in_specs=[pl.BlockSpec(memory_space=pltpu.SMEM), pl.BlockSpec(memory_space=pltpu.HBM)],
        out_specs=[whole, whole],
        scratch_shapes=[
            pltpu.VMEM((rows, slots, 1, width), jnp.float32),
            pltpu.SemaphoreType.DMA,
        ],
        compiler_params=pltpu.CompilerParams(vmem_limit_bytes=65500000),
        name="copies",
    )(start[None], window)


def to_all(piece, axis, peers, groups=None):
    copies = jnp.broadcast_to(piece[None], (peers, *piece.shape))
    return lax.all_to_all(copies, axis, 0, 0, axis_index_groups=groups)


def local(schur_window):
    row_blocks, _, width, col_blocks, _, _ = schur_window.shape
    held = schur_window.reshape(row_blocks, width, col_blocks, width)
    layers = lax.axis_size("layer")
    grid_rows = lax.axis_size("row")
    grid_cols = lax.axis_size("col")
    layer_here = lax.axis_index("layer")
    row_here = lax.axis_index("row")
    col_here = lax.axis_index("col")
    x_size = layers // 2
    x_groups = [[x * 2 + z for x in range(x_size)] for z in range(2)]
    share = width // layers
    quarter = width // x_size
    lead = PANELS * width

    parts = copies(layer_here // 2, schur_window, grid_rows, quarter)

    def collect(part):
        quarters = lax.all_to_all(part, "row", 0, 0)[:PANELS]
        gathered = to_all(quarters, "layer", x_size, x_groups)
        return jnp.moveaxis(gathered, 0, 1).reshape(lead, -1)

    lead_part = collect(parts[0])
    rest_part = collect(parts[1])
    mine = lax.dynamic_slice_in_dim(held, layer_here * share, share, 1)
    mine_first = mine[:, :, 0, :].reshape(row_blocks * share, width)
    swapped_in = jnp.concatenate([lead_part, mine_first], axis=0)
    swapped = lax.ppermute(swapped_in, "col", [(0, 1), (1, 0)])
    panel, half = weigh(col_here[None], swapped_in, swapped)
    far = lax.ppermute(half, "col", [(0, 4), (1, 5)])
    half = jnp.where(col_here < 4, half, far)
    near = lax.ppermute(half, "col", [(0, 2), (1, 3), (4, 6), (5, 7)])
    half = jnp.where(col_here % 4 < 2, half, near)
    other = lax.ppermute(half, "col", [(i, i ^ 1) for i in range(grid_cols)])
    is_even = col_here % 2 == 0
    weights_here = jnp.concatenate(
        [jnp.where(is_even, half, other), jnp.where(is_even, other, half)], axis=1
    )
    update = product(weights_here, jnp.concatenate([lead_part, rest_part], axis=1))
    trailing = mine - update.reshape(row_blocks, share, col_blocks, width)

    row_number = (jnp.arange(row_blocks, dtype=jnp.int32) * grid_rows + row_here)[:, None, None, None]
    col_number = (jnp.arange(col_blocks, dtype=jnp.int32) * grid_cols + col_here)[None, None, :, None]
    row_inside = (jnp.arange(share, dtype=jnp.int32) + layer_here * share)[None, :, None, None]
    col_inside = jnp.arange(width, dtype=jnp.int32)[None, None, None, :]
    panel = panel.reshape(row_blocks, share, 1, width)
    below = (row_number > col_number) | ((row_number == col_number) & (row_inside >= col_inside))
    panel = jnp.where(below, panel, 0.0)
    trailing = jnp.where(row_number < PANELS, 0.0, trailing)
    result = jnp.where(col_number < PANELS, panel, trailing)
    return result.reshape(row_blocks, 1, share, col_blocks, 1, width)


def solution(mesh):
    return jax.shard_map(
        local,
        mesh=mesh,
        in_specs=(P(None, "row", None, None, "col", None),),
        out_specs=P(None, "row", "layer", None, "col", None),
        check_vma=False,
    )
```

```python
import functools
import jax
import jax.numpy as jnp
from jax import lax
from jax.experimental import pallas as pl
from jax.experimental.pallas import tpu as pltpu
from jax.sharding import PartitionSpec as P

PANELS = 2
BLOCK = 128
STRIP = 64
HIGHEST = lax.Precision.HIGHEST


def product(left, right, dims=((1,), (0,))):
    return lax.dot_general(left, right, (dims, ((), ())), precision=HIGHEST, preferred_element_type=jnp.float32)


def spread_lane(part, lane, sublane):
    return jnp.where(sublane < 8, jnp.broadcast_to(part[:, lane : lane + 1], (8, 128)), 0.0)


def eliminate(groups, first_lane, work):
    count = len(groups)
    sublane = lax.broadcasted_iota(jnp.int32, (8, 128), 0)
    lane_id = lax.broadcasted_iota(jnp.int32, (8, 128), 1)
    parts = list(groups)
    def spread(i, lane, guard):
        if guard:
            return [spread_lane(parts[i], lane + s, sublane) for s in range(8)]
        return [jnp.broadcast_to(parts[i][:, lane + s : lane + s + 1], (8, 128)) for s in range(8)]
    current = spread(0, first_lane, True)
    for g in range(count):
        lane = first_lane + 8 * g
        more = g + 1 < count
        heads = [current + (spread(g, lane + 8, True) if more else [])]
        if more:
            heads.append(spread(g + 1, lane, False) + spread(g + 1, lane + 8, True))
        for i in range(g + 2, count):
            heads.append(spread(i, lane, False))
        inside = (lane_id >= lane) & (lane_id < lane + 8)
        unit = (lane_id - lane == sublane).astype(jnp.float32)
        for i in range(g, count):
            parts[i] = jnp.where(inside, unit if i == g else 0.0, parts[i])
        scale = None
        for s in range(8):
            below = jnp.where(sublane > s, heads[0][s], 0.0)
            head_rows = [
                jnp.broadcast_to(head[s : s + 1, :], (8, 128)) for head in heads[0][s + 1 :]
            ]
            root = lax.rsqrt(jnp.broadcast_to(heads[0][s][s : s + 1, :], (8, 128)))
            inverse = root * root
            scale = root if s == 0 else jnp.where(sublane == s, root, scale)
            row = jnp.broadcast_to(parts[g][s : s + 1, :], (8, 128))
            if s < 7:
                heads[0][s + 1] = heads[0][s + 1] - (below * head_rows[0]) * inverse
            for i in range(g, count):
                if i == g and s == 7:
                    continue
                factor = (below if i == g else heads[i - g][s]) * inverse
                parts[i] = parts[i] - factor * row
                for p in range(s + 1, len(heads[i - g])):
                    if i > g or p > s + 1:
                        heads[i - g][p] = heads[i - g][p] - factor * head_rows[p - s - 1]
        parts[g] = parts[g] * scale
        if more:
            current = heads[1][8:]
        work()
    return jnp.concatenate(parts, axis=0)


def factor_body(
    first, mine_ref, other_ref, panel_ref, half_ref, v_ref, x_ref, w_ref, p_ref, e_ref, block_ref
):
    size = w_ref.shape[0]
    half = size // 2
    count = size // BLOCK
    def left(rows):
        return jnp.where(first, mine_ref[rows, :], other_ref[rows, :])
    def right(rows):
        return jnp.where(first, other_ref[rows, :], mine_ref[rows, :])
    w_ref[:half, :half] = left(slice(0, half))
    w_ref[:, half:] = right(slice(0, size))
    p_ref[:half, :] = left(slice(size, None)).T
    p_ref[half:, :] = right(slice(size, None)).T
    row_id = lax.broadcasted_iota(jnp.int32, (BLOCK, BLOCK), 0)
    col_id = lax.broadcasted_iota(jnp.int32, (BLOCK, BLOCK), 1)
    at = [slice(k * BLOCK, (k + 1) * BLOCK) for k in range(count)]
    pending = []
    for k in range(count):
        slots = 2 * STRIP // 8
        per = -(-len(pending) // (slots - 2)) if pending else 0
        def work():
            for _ in range(per):
                if pending:
                    pending.pop(0)()
        block_ref[...] = w_ref[at[k], at[k]]
        for begin in range(0, BLOCK, STRIP):
            end = begin + STRIP
            groups = [block_ref[begin + 8 * i : begin + 8 * i + 8, :] for i in range(STRIP // 8)]
            done = eliminate(groups, begin, work)
            rows, lanes = row_id[begin:end], col_id[begin:end]
            block_ref[begin:end, :] = jnp.where(lanes <= rows, done, 0.0)
            if end < BLOCK:
                done = jnp.where((lanes <= rows) | (lanes >= end), done, 0.0)
                rest = block_ref[end:, :]
                rest = jnp.where((col_id[end:] >= begin) & (col_id[end:] < end), 0.0, rest)
                block_ref[end:, :] = rest - product(done.T[end:], done)
        while pending:
            pending.pop(0)()
        e_ref[at[k], at[k]] = block_ref[...]
        if k < count - 1:
            inverse = block_ref[...]
            upper = product(inverse, w_ref[at[k], at[k + 1]])
            w_ref[at[k], at[k + 1]] = upper
            w_ref[at[k + 1], at[k + 1]] -= product(upper.T, upper)
            def panel(k=k, j=0):
                w_ref[at[k], at[j]] = product(e_ref[at[k], at[k]], w_ref[at[k], at[j]])
            def panel_p(k=k):
                p_ref[at[k], :] = product(e_ref[at[k], at[k]], p_ref[at[k], :])
            def panel_e(k=k):
                e_ref[at[k], : k * BLOCK] = product(e_ref[at[k], at[k]], e_ref[at[k], : k * BLOCK])
            def trail(k=k, i=0, j=0):
                w_ref[at[i], at[j]] -= product(w_ref[at[k], at[i]].T, w_ref[at[k], at[j]])
            def trail_p(k=k, i=0):
                p_ref[at[i], :] -= product(w_ref[at[k], at[i]].T, p_ref[at[k], :])
            def trail_e(k=k, i=0):
                lower = w_ref[at[k], at[i]].T
                e_ref[at[i], at[k]] = -product(lower, e_ref[at[k], at[k]])
                if k > 0:
                    e_ref[at[i], : k * BLOCK] -= product(lower, e_ref[at[k], : k * BLOCK])
            def output(k=k):
                solved = p_ref[at[k], :].T
                v_ref[:, at[k]] = solved
                x_ref[:, at[k]] = product(solved, e_ref[at[k], at[k]])
                if k > 0:
                    x_ref[:, : k * BLOCK] += product(solved, e_ref[at[k], : k * BLOCK])
            bind = functools.partial
            for j in range(k + 2, count):
                pending.append(bind(panel, j=j))
            pending.append(panel_p)
            for i in range(k + 1, count):
                for j in range(i, count):
                    if j > k + 1:
                        pending.append(bind(trail, i=i, j=j))
                pending.append(bind(trail_p, i=i))
            if k > 0:
                pending.append(panel_e)
            for i in range(k + 1, count):
                pending.append(bind(trail_e, i=i))
            pending.append(output)
    last = at[count - 1]
    inverse = block_ref[...]
    solved = product(p_ref[last, :], inverse, ((0,), (1,)))
    v_ref[:, last] = solved
    weights = product(solved, inverse)
    x_ref[:, last] = weights
    x_ref[:, : size - BLOCK] += product(weights, e_ref[last, : size - BLOCK])
    panel_ref[...] = jnp.where(first, v_ref[:, :half], v_ref[:, half:])
    half_ref[...] = jnp.where(first, x_ref[:, :half], x_ref[:, half:])


def factor_kernel(position_ref, mine_ref, other_ref, panel_ref, half_ref, *scratch):
    position = position_ref[0]

    @pl.when(position < 2)
    def _():
        factor_body(position == 0, mine_ref, other_ref, panel_ref, half_ref, *scratch)

    @pl.when(position >= 2)
    def _():
        panel_ref[...] = jnp.zeros_like(panel_ref)
        half_ref[...] = jnp.zeros_like(half_ref)


def weigh(position, mine, other):
    size = 2 * mine.shape[1]
    share = mine.shape[0] - size
    shape = jax.ShapeDtypeStruct((share, size // 2), jnp.float32)
    whole = pl.BlockSpec(memory_space=pltpu.VMEM)
    return pl.pallas_call(
        factor_kernel,
        out_shape=[shape, shape],
        in_specs=[pl.BlockSpec(memory_space=pltpu.SMEM), whole, whole],
        out_specs=[whole, whole],
        scratch_shapes=[
            pltpu.VMEM((share, size), jnp.float32),
            pltpu.VMEM((share, size), jnp.float32),
            pltpu.VMEM((size, size), jnp.float32),
            pltpu.VMEM((size, share), jnp.float32),
            pltpu.VMEM((size, size), jnp.float32),
            pltpu.VMEM((BLOCK, BLOCK), jnp.float32),
        ],
        compiler_params=pltpu.CompilerParams(vmem_limit_bytes=16 << 20),
        name="factor",
    )(position, mine, other)


def copies_kernel(start_ref, window_ref, lead_ref, rest_ref, part_ref, arrived):
    rows = part_ref.shape[0]
    begin = pl.multiple_of(start_ref[0] * rows, rows)
    copy = pltpu.make_async_copy(window_ref.at[0, 0, pl.ds(begin, rows)], part_ref, arrived)
    copy.start()
    copy.wait()
    for slot, out_ref in enumerate((lead_ref, rest_ref)):
        part = part_ref[:, slot, 0, :]
        for peer in range(out_ref.shape[0]):
            out_ref[peer] = part


def copies(start, window, peers, rows):
    slots, width = window.shape[3], window.shape[5]
    shape = jax.ShapeDtypeStruct((peers, rows, width), jnp.float32)
    whole = pl.BlockSpec(memory_space=pltpu.VMEM)
    return pl.pallas_call(
        copies_kernel,
        out_shape=[shape, shape],
        in_specs=[pl.BlockSpec(memory_space=pltpu.SMEM), pl.BlockSpec(memory_space=pltpu.HBM)],
        out_specs=[whole, whole],
        scratch_shapes=[
            pltpu.VMEM((rows, slots, 1, width), jnp.float32),
            pltpu.SemaphoreType.DMA,
        ],
        compiler_params=pltpu.CompilerParams(vmem_limit_bytes=65500000),
        name="copies",
    )(start[None], window)


def to_all(piece, axis, peers, groups=None):
    copies = jnp.broadcast_to(piece[None], (peers, *piece.shape))
    return lax.all_to_all(copies, axis, 0, 0, axis_index_groups=groups)


def local(schur_window):
    row_blocks, _, width, col_blocks, _, _ = schur_window.shape
    held = schur_window.reshape(row_blocks, width, col_blocks, width)
    layers = lax.axis_size("layer")
    grid_rows = lax.axis_size("row")
    grid_cols = lax.axis_size("col")
    layer_here = lax.axis_index("layer")
    row_here = lax.axis_index("row")
    col_here = lax.axis_index("col")
    x_size = layers // 2
    x_groups = [[x * 2 + z for x in range(x_size)] for z in range(2)]
    share = width // layers
    quarter = width // x_size
    lead = PANELS * width

    parts = copies(layer_here // 2, schur_window, grid_rows, quarter)

    def across_x(quarters):
        gathered = to_all(quarters, "layer", x_size, x_groups)
        return jnp.moveaxis(gathered, 0, 1).reshape(lead, -1)

    quarters = lax.all_to_all(parts[0], "row", 0, 0)[:PANELS]
    lead_part = across_x(quarters)
    part = parts[1][0]
    other = lax.ppermute(part, "row", [(0, 1), (1, 0)])
    is_top = row_here == 0
    quarters = jnp.stack([jnp.where(is_top, part, other), jnp.where(is_top, other, part)])
    received = lax.ppermute(quarters, "row", [(0, 6), (1, 3)])
    quarters = jnp.where(row_here < PANELS, quarters, received)
    received = lax.ppermute(quarters, "row", [(0, 7), (1, 2), (6, 5), (3, 4)])
    holds = (row_here < PANELS) | (row_here == 3) | (row_here == 6)
    quarters = jnp.where(holds, quarters, received)
    rest_part = across_x(quarters)

    mine = lax.dynamic_slice_in_dim(held, layer_here * share, share, 1)
    mine_first = mine[:, :, 0, :].reshape(row_blocks * share, width)
    swapped_in = jnp.concatenate([lead_part, mine_first], axis=0)
    swapped = lax.ppermute(swapped_in, "col", [(0, 1), (1, 0)])
    panel, half = weigh(col_here[None], swapped_in, swapped)
    far = lax.ppermute(half, "col", [(0, 4), (1, 5)])
    half = jnp.where(col_here < 4, half, far)
    near = lax.ppermute(half, "col", [(0, 2), (1, 3), (4, 6), (5, 7)])
    half = jnp.where(col_here % 4 < 2, half, near)
    other = lax.ppermute(half, "col", [(i, i ^ 1) for i in range(grid_cols)])
    is_even = col_here % 2 == 0
    weights_here = jnp.concatenate(
        [jnp.where(is_even, half, other), jnp.where(is_even, other, half)], axis=1
    )
    update = product(weights_here, jnp.concatenate([lead_part, rest_part], axis=1))
    trailing = mine - update.reshape(row_blocks, share, col_blocks, width)

    row_number = (jnp.arange(row_blocks, dtype=jnp.int32) * grid_rows + row_here)[:, None, None, None]
    col_number = (jnp.arange(col_blocks, dtype=jnp.int32) * grid_cols + col_here)[None, None, :, None]
    row_inside = (jnp.arange(share, dtype=jnp.int32) + layer_here * share)[None, :, None, None]
    col_inside = jnp.arange(width, dtype=jnp.int32)[None, None, None, :]
    panel = panel.reshape(row_blocks, share, 1, width)
    below = (row_number > col_number) | ((row_number == col_number) & (row_inside >= col_inside))
    panel = jnp.where(below, panel, 0.0)
    trailing = jnp.where(row_number < PANELS, 0.0, trailing)
    result = jnp.where(col_number < PANELS, panel, trailing)
    return result.reshape(row_blocks, 1, share, col_blocks, 1, width)


def solution(mesh):
    return jax.shard_map(
        local,
        mesh=mesh,
        in_specs=(P(None, "row", None, None, "col", None),),
        out_specs=P(None, "row", "layer", None, "col", None),
        check_vma=False,
    )
```

```python
import functools
import jax
import jax.numpy as jnp
from jax import lax
from jax.experimental import pallas as pl
from jax.experimental.pallas import tpu as pltpu
from jax.sharding import PartitionSpec as P

PANELS = 2
BLOCK = 128
STRIP = 64
HIGHEST = lax.Precision.HIGHEST


def product(left, right, dims=((1,), (0,))):
    return lax.dot_general(left, right, (dims, ((), ())), precision=HIGHEST, preferred_element_type=jnp.float32)


def spread_lane(part, lane, sublane):
    return jnp.where(sublane < 8, jnp.broadcast_to(part[:, lane : lane + 1], (8, 128)), 0.0)


def eliminate(groups, first_lane, work):
    count = len(groups)
    sublane = lax.broadcasted_iota(jnp.int32, (8, 128), 0)
    lane_id = lax.broadcasted_iota(jnp.int32, (8, 128), 1)
    parts = list(groups)
    def spread(i, lane, guard):
        if guard:
            return [spread_lane(parts[i], lane + s, sublane) for s in range(8)]
        return [jnp.broadcast_to(parts[i][:, lane + s : lane + s + 1], (8, 128)) for s in range(8)]
    current = spread(0, first_lane, True)
    for g in range(count):
        lane = first_lane + 8 * g
        more = g + 1 < count
        heads = [current + (spread(g, lane + 8, True) if more else [])]
        if more:
            heads.append(spread(g + 1, lane, False) + spread(g + 1, lane + 8, True))
        for i in range(g + 2, count):
            heads.append(spread(i, lane, False))
        inside = (lane_id >= lane) & (lane_id < lane + 8)
        unit = (lane_id - lane == sublane).astype(jnp.float32)
        for i in range(g, count):
            parts[i] = jnp.where(inside, unit if i == g else 0.0, parts[i])
        scale = None
        for s in range(8):
            below = jnp.where(sublane > s, heads[0][s], 0.0)
            head_rows = [
                jnp.broadcast_to(head[s : s + 1, :], (8, 128)) for head in heads[0][s + 1 :]
            ]
            root = lax.rsqrt(jnp.broadcast_to(heads[0][s][s : s + 1, :], (8, 128)))
            inverse = root * root
            scale = root if s == 0 else jnp.where(sublane == s, root, scale)
            row = jnp.broadcast_to(parts[g][s : s + 1, :], (8, 128))
            if s < 7:
                heads[0][s + 1] = heads[0][s + 1] - (below * head_rows[0]) * inverse
            for i in range(g, count):
                if i == g and s == 7:
                    continue
                factor = (below if i == g else heads[i - g][s]) * inverse
                parts[i] = parts[i] - factor * row
                for p in range(s + 1, len(heads[i - g])):
                    if i > g or p > s + 1:
                        heads[i - g][p] = heads[i - g][p] - factor * head_rows[p - s - 1]
        parts[g] = parts[g] * scale
        if more:
            current = heads[1][8:]
        work()
    return jnp.concatenate(parts, axis=0)


def factor_body(
    first, mine_ref, other_ref, panel_ref, half_ref, v_ref, x_ref, w_ref, p_ref, e_ref, block_ref
):
    size = w_ref.shape[0]
    half = size // 2
    count = size // BLOCK
    def left(rows):
        return jnp.where(first, mine_ref[rows, :], other_ref[rows, :])
    def right(rows):
        return jnp.where(first, other_ref[rows, :], mine_ref[rows, :])
    w_ref[:half, :half] = left(slice(0, half))
    w_ref[:, half:] = right(slice(0, size))
    p_ref[:half, :] = left(slice(size, None)).T
    p_ref[half:, :] = right(slice(size, None)).T
    row_id = lax.broadcasted_iota(jnp.int32, (BLOCK, BLOCK), 0)
    col_id = lax.broadcasted_iota(jnp.int32, (BLOCK, BLOCK), 1)
    at = [slice(k * BLOCK, (k + 1) * BLOCK) for k in range(count)]
    pending = []
    for k in range(count):
        slots = 2 * STRIP // 8
        per = -(-len(pending) // (slots - 2)) if pending else 0
        def work():
            for _ in range(per):
                if pending:
                    pending.pop(0)()
        block_ref[...] = w_ref[at[k], at[k]]
        for begin in range(0, BLOCK, STRIP):
            end = begin + STRIP
            groups = [block_ref[begin + 8 * i : begin + 8 * i + 8, :] for i in range(STRIP // 8)]
            done = eliminate(groups, begin, work)
            rows, lanes = row_id[begin:end], col_id[begin:end]
            block_ref[begin:end, :] = jnp.where(lanes <= rows, done, 0.0)
            if end < BLOCK:
                done = jnp.where((lanes <= rows) | (lanes >= end), done, 0.0)
                rest = block_ref[end:, :]
                rest = jnp.where((col_id[end:] >= begin) & (col_id[end:] < end), 0.0, rest)
                block_ref[end:, :] = rest - product(done.T[end:], done)
        while pending:
            pending.pop(0)()
        e_ref[at[k], at[k]] = block_ref[...]
        if k < count - 1:
            inverse = block_ref[...]
            upper = product(inverse, w_ref[at[k], at[k + 1]])
            w_ref[at[k], at[k + 1]] = upper
            w_ref[at[k + 1], at[k + 1]] -= product(upper.T, upper)
            def panel(k=k, j=0):
                w_ref[at[k], at[j]] = product(e_ref[at[k], at[k]], w_ref[at[k], at[j]])
            def panel_p(k=k):
                p_ref[at[k], :] = product(e_ref[at[k], at[k]], p_ref[at[k], :])
            def panel_e(k=k):
                e_ref[at[k], : k * BLOCK] = product(e_ref[at[k], at[k]], e_ref[at[k], : k * BLOCK])
            def trail(k=k, i=0, j=0):
                w_ref[at[i], at[j]] -= product(w_ref[at[k], at[i]].T, w_ref[at[k], at[j]])
            def trail_p(k=k, i=0):
                p_ref[at[i], :] -= product(w_ref[at[k], at[i]].T, p_ref[at[k], :])
            def trail_e(k=k, i=0):
                lower = w_ref[at[k], at[i]].T
                e_ref[at[i], at[k]] = -product(lower, e_ref[at[k], at[k]])
                if k > 0:
                    e_ref[at[i], : k * BLOCK] -= product(lower, e_ref[at[k], : k * BLOCK])
            def output(k=k):
                solved = p_ref[at[k], :].T
                v_ref[:, at[k]] = solved
                x_ref[:, at[k]] = product(solved, e_ref[at[k], at[k]])
                if k > 0:
                    x_ref[:, : k * BLOCK] += product(solved, e_ref[at[k], : k * BLOCK])
            bind = functools.partial
            for j in range(k + 2, count):
                pending.append(bind(panel, j=j))
            pending.append(panel_p)
            for i in range(k + 1, count):
                for j in range(i, count):
                    if j > k + 1:
                        pending.append(bind(trail, i=i, j=j))
                pending.append(bind(trail_p, i=i))
            if k > 0:
                pending.append(panel_e)
            for i in range(k + 1, count):
                pending.append(bind(trail_e, i=i))
            pending.append(output)
    last = at[count - 1]
    inverse = block_ref[...]
    solved = product(p_ref[last, :], inverse, ((0,), (1,)))
    v_ref[:, last] = solved
    weights = product(solved, inverse)
    x_ref[:, last] = weights
    x_ref[:, : size - BLOCK] += product(weights, e_ref[last, : size - BLOCK])
    panel_ref[...] = jnp.where(first, v_ref[:, :half], v_ref[:, half:])
    half_ref[...] = jnp.where(first, x_ref[:, :half], x_ref[:, half:])


def factor_kernel(position_ref, mine_ref, other_ref, panel_ref, half_ref, *scratch):
    position = position_ref[0]

    @pl.when(position < 2)
    def _():
        factor_body(position == 0, mine_ref, other_ref, panel_ref, half_ref, *scratch)

    @pl.when(position >= 2)
    def _():
        panel_ref[...] = jnp.zeros_like(panel_ref)
        half_ref[...] = jnp.zeros_like(half_ref)


def weigh(position, mine, other):
    size = 2 * mine.shape[1]
    share = mine.shape[0] - size
    shape = jax.ShapeDtypeStruct((share, size // 2), jnp.float32)
    whole = pl.BlockSpec(memory_space=pltpu.VMEM)
    return pl.pallas_call(
        factor_kernel,
        out_shape=[shape, shape],
        in_specs=[pl.BlockSpec(memory_space=pltpu.SMEM), whole, whole],
        out_specs=[whole, whole],
        scratch_shapes=[
            pltpu.VMEM((share, size), jnp.float32),
            pltpu.VMEM((share, size), jnp.float32),
            pltpu.VMEM((size, size), jnp.float32),
            pltpu.VMEM((size, share), jnp.float32),
            pltpu.VMEM((size, size), jnp.float32),
            pltpu.VMEM((BLOCK, BLOCK), jnp.float32),
        ],
        compiler_params=pltpu.CompilerParams(vmem_limit_bytes=16 << 20),
        name="factor",
    )(position, mine, other)


def copies_kernel(start_ref, window_ref, lead_ref, rest_ref, part_ref, arrived):
    rows = part_ref.shape[0]
    begin = pl.multiple_of(start_ref[0] * rows, rows)
    copy = pltpu.make_async_copy(window_ref.at[0, 0, pl.ds(begin, rows)], part_ref, arrived)
    copy.start()
    copy.wait()
    rest_ref[...] = part_ref[:, 1, 0, :]
    part = part_ref[:, 0, 0, :]
    for peer in range(lead_ref.shape[0]):
        lead_ref[peer] = part


def copies(start, window, peers, rows):
    slots, width = window.shape[3], window.shape[5]
    shapes = [(peers, rows, width), (rows, width)]
    whole = pl.BlockSpec(memory_space=pltpu.VMEM)
    return pl.pallas_call(
        copies_kernel,
        out_shape=[jax.ShapeDtypeStruct(shape, jnp.float32) for shape in shapes],
        in_specs=[pl.BlockSpec(memory_space=pltpu.SMEM), pl.BlockSpec(memory_space=pltpu.HBM)],
        out_specs=[whole, whole],
        scratch_shapes=[
            pltpu.VMEM((rows, slots, 1, width), jnp.float32),
            pltpu.SemaphoreType.DMA,
        ],
        compiler_params=pltpu.CompilerParams(vmem_limit_bytes=65500000),
        name="copies",
    )(start[None], window)


def to_all(piece, axis, peers, groups=None):
    copies = jnp.broadcast_to(piece[None], (peers, *piece.shape))
    return lax.all_to_all(copies, axis, 0, 0, axis_index_groups=groups)


def local(schur_window):
    row_blocks, _, width, col_blocks, _, _ = schur_window.shape
    held = schur_window.reshape(row_blocks, width, col_blocks, width)
    layers = lax.axis_size("layer")
    grid_rows = lax.axis_size("row")
    grid_cols = lax.axis_size("col")
    layer_here = lax.axis_index("layer")
    row_here = lax.axis_index("row")
    col_here = lax.axis_index("col")
    x_size = layers // 2
    x_groups = [[x * 2 + z for x in range(x_size)] for z in range(2)]
    share = width // layers
    quarter = width // x_size
    lead = PANELS * width

    parts = copies(layer_here // 2, schur_window, grid_rows, quarter)

    def across_x(quarters):
        gathered = to_all(quarters, "layer", x_size, x_groups)
        return jnp.moveaxis(gathered, 0, 1).reshape(lead, -1)

    quarters = lax.all_to_all(parts[0], "row", 0, 0)[:PANELS]
    lead_part = across_x(quarters)
    part = parts[1]
    other = lax.ppermute(part, "row", [(0, 1), (1, 0)])
    is_top = row_here == 0
    quarters = jnp.stack([jnp.where(is_top, part, other), jnp.where(is_top, other, part)])
    received = lax.ppermute(quarters, "row", [(0, 6), (1, 3)])
    quarters = jnp.where(row_here < PANELS, quarters, received)
    received = lax.ppermute(quarters, "row", [(0, 7), (1, 2), (6, 5), (3, 4)])
    holds = (row_here < PANELS) | (row_here == 3) | (row_here == 6)
    quarters = jnp.where(holds, quarters, received)
    rest_part = across_x(quarters)

    mine = lax.dynamic_slice_in_dim(held, layer_here * share, share, 1)
    mine_first = mine[:, :, 0, :].reshape(row_blocks * share, width)
    swapped_in = jnp.concatenate([lead_part, mine_first], axis=0)
    swapped = lax.ppermute(swapped_in, "col", [(0, 1), (1, 0)])
    panel, half = weigh(col_here[None], swapped_in, swapped)
    far = lax.ppermute(half, "col", [(0, 4), (1, 5)])
    half = jnp.where(col_here < 4, half, far)
    near = lax.ppermute(half, "col", [(0, 2), (1, 3), (4, 6), (5, 7)])
    half = jnp.where(col_here % 4 < 2, half, near)
    other = lax.ppermute(half, "col", [(i, i ^ 1) for i in range(grid_cols)])
    is_even = col_here % 2 == 0
    weights_here = jnp.concatenate(
        [jnp.where(is_even, half, other), jnp.where(is_even, other, half)], axis=1
    )
    update = product(weights_here, jnp.concatenate([lead_part, rest_part], axis=1))
    trailing = mine - update.reshape(row_blocks, share, col_blocks, width)

    row_number = (jnp.arange(row_blocks, dtype=jnp.int32) * grid_rows + row_here)[:, None, None, None]
    col_number = (jnp.arange(col_blocks, dtype=jnp.int32) * grid_cols + col_here)[None, None, :, None]
    row_inside = (jnp.arange(share, dtype=jnp.int32) + layer_here * share)[None, :, None, None]
    col_inside = jnp.arange(width, dtype=jnp.int32)[None, None, None, :]
    panel = panel.reshape(row_blocks, share, 1, width)
    below = (row_number > col_number) | ((row_number == col_number) & (row_inside >= col_inside))
    panel = jnp.where(below, panel, 0.0)
    trailing = jnp.where(row_number < PANELS, 0.0, trailing)
    result = jnp.where(col_number < PANELS, panel, trailing)
    return result.reshape(row_blocks, 1, share, col_blocks, 1, width)


def solution(mesh):
    return jax.shard_map(
        local,
        mesh=mesh,
        in_specs=(P(None, "row", None, None, "col", None),),
        out_specs=P(None, "row", "layer", None, "col", None),
        check_vma=False,
    )
```
